32 devices in a mesh: query: 4 (over y, x), corpus: 8 (over z, core).
Axes of the slice: x: 2, y: 2, z: 4, core: 2. Of those that a mesh axis runs over, the one named last changes fastest.
Arguments:
- hidden_in: bfloat16 [512, 4096], P('query', 'corpus'), may hold values from -6 to 6
- lengths: int32 [16], P('query'), may hold values from 1 to 32, 320 in all
- gate_weight: bfloat16 [4096, 14336], P('query', 'corpus'), may hold values from -0.09375 to 0.09375
- up_weight: bfloat16 [4096, 14336], P('query', 'corpus'), may hold values from -0.09375 to 0.09375
- down_weight: bfloat16 [14336, 4096], P('corpus', 'query'), may hold values from -0.04175957 to 0.04175957
- code_weight: bfloat16 [4096, 1024], P('corpus'), may hold values from -0.03125 to 0.03125
- corpus_codes: bfloat16 [16384, 1024], P(('query', 'corpus')), may hold values from -1 to 1, as said below
Outputs:
- top_scores: float32 [16, 100], replicated
The draws below stay inside these ranges and needn't reach their ends.
Inputs may be any that keep to these rules, and one draw needn't show every extreme that they name: `corpus_codes`: every entry is +1 or -1. `lengths`: at least one query has all 32 slots real.
All inputs are finite; a program needn't handle non-finite values. No bound on the sum of `lengths` on one device may be relied on, other than what follows from the above.
Results may differ from the reference program's by a relative error of at most 0.00067.
Values may be sent and summed in bfloat16 or wider, within the bound.
A program may use at most 128 MiB of HBM per device.

```python
import math
import jax
import jax.numpy as jnp
import numpy as np
from jax import lax

D = 4096
FF = 14336
BITS = 1024
SEQ = 32
TOPK = 100
DOCS_DEV = 512
QUERIES = 16
TOKENS = 512
DOCS = 16384


def shared_parts(key):
    offset = 1.2 * jnp.clip(jax.random.normal(jax.random.fold_in(key, 101), (D,), jnp.float32), -2.5, 2.5)
    bound = 2.0 / max(8, D // 64)
    code_matrix = jax.random.uniform(jax.random.fold_in(key, 102), (D, BITS), jnp.float32, -bound, bound)
    return (offset, code_matrix)


def draw_code_weight(key, part):
    offset, code_matrix = shared_parts(key)
    return code_matrix.astype(jnp.bfloat16)


def draw_down_weight(key, part):
    unit_scale = FF ** (-0.5)
    noise_part = jnp.clip(jax.random.normal(jax.random.fold_in(key, 201), (FF, D), jnp.float32), -3.0, 3.0)
    sign_table = jnp.where(jax.random.uniform(jax.random.fold_in(key, 202), (FF, 1), jnp.float32) < 0.5, -1.0, 1.0)
    directions = jax.random.uniform(jax.random.fold_in(key, 203), (1, D), jnp.float32, -1.7, 1.7)
    common_part = sign_table * directions
    combined = (noise_part + common_part) * unit_scale
    return jnp.clip(combined, -5.0 * unit_scale, 5.0 * unit_scale).astype(jnp.bfloat16)


def draw_hidden_in(key, part):
    offset, code_matrix = shared_parts(key)
    noise_key = jax.random.fold_in(key, 103)
    noise = jnp.clip(jax.random.normal(noise_key, (TOKENS, D), jnp.float32), -4.0, 4.0)
    return jnp.clip(noise + offset[None, :], -6.0, 6.0).astype(jnp.bfloat16)


def draw_corpus_codes(key, part):
    offset, code_matrix = shared_parts(key)
    rounded = code_matrix.astype(jnp.bfloat16).astype(jnp.float32)
    direction = jnp.dot(offset, rounded, precision=lax.Precision.HIGHEST)
    sign_code = jnp.where(direction >= 0.0, 1.0, -1.0).astype(jnp.float32)
    flips = jax.random.uniform(jax.random.fold_in(key, 17), (DOCS, BITS), jnp.float32)
    chosen = jax.random.randint(jax.random.fold_in(key, 18), (), 0, DOCS // DOCS_DEV)
    placing = jax.random.permutation(jax.random.fold_in(key, 19), DOCS_DEV).astype(jnp.int32)
    rows = jnp.arange(DOCS, dtype=jnp.int32)
    planted = jnp.logical_and(rows // DOCS_DEV == chosen, placing[rows % DOCS_DEV] < TOPK // 2)
    rates = jax.random.uniform(jax.random.fold_in(key, 20), (DOCS, 1), jnp.float32, 0.2, 0.5)
    near_copy = sign_code[None, :] * jnp.where(flips < rates, -1.0, 1.0)
    drawn = jnp.where(flips < 0.5, 1.0, -1.0)
    return jnp.where(planted[:, None], near_copy, drawn).astype(jnp.float32).astype(jnp.bfloat16)


def steps_of(key, extent, cuts, smallest, largest):
    loudness = 1.0
    for dim, parts in cuts:
        draws = jax.random.uniform(jax.random.fold_in(jax.random.fold_in(key, 6), dim), (parts,), jnp.float32, smallest / len(cuts), largest / len(cuts))
        loudness = loudness * jnp.repeat(jnp.exp(draws), extent[dim] // parts).reshape((-1,) + (1,) * (len(extent) - 1 - dim))
    return loudness


def split_up(count, total, limit, skew):
    portions = [(1 << 20) // math.isqrt(standing ** skew) + 1 for standing in range(2, count + 1)]
    surplus, counts = total - limit - (count - 1), [1] * (count - 1)
    while surplus > 0:
        movable = [i for i in range(count - 1) if counts[i] < limit]
        mass, budget = sum([portions[i] for i in movable]), surplus
        for i in movable:
            addition = min(limit - counts[i], max(1, budget * portions[i] // mass), surplus)
            counts[i] = counts[i] + addition
            surplus = surplus - addition
    return np.array([limit] + counts)


def uneven_parts(rng, amount, total, most, lean):
    if amount == 2:
        one = jax.random.randint(rng, (), max(1, total - most), min(most, total - 1) + 1)
        return jnp.stack([one, total - one])
    sizes = jnp.asarray(split_up(amount, total, most, lean), jnp.int32)
    twos = (amount - 1) // 2
    giver, taker = sizes[1:1 + 2 * twos:2], sizes[2:2 + 2 * twos:2]
    margin = jnp.minimum(giver - 1, most - taker)
    shifted = jax.random.randint(jax.random.fold_in(rng, 1), (twos,), 0, 1 << 20) % (margin + 1)
    sizes = sizes.at[1:1 + 2 * twos:2].set(giver - shifted).at[2:2 + 2 * twos:2].set(taker + shifted)
    return sizes[jax.random.permutation(jax.random.fold_in(rng, 2), amount)]


def centred(own_key, shape, scale, reach, pieces=(), held_as=jnp.bfloat16):
    result = scale * jax.random.normal(own_key, shape, jnp.float32)
    if pieces:
        result = result * steps_of(own_key, shape, pieces, -0.22, 0.18)
    return jnp.clip(result, -reach, reach).astype(held_as)


def setup_inputs(seed: int = 0) -> dict:
    arg_keys = jax.random.split(jax.random.key(seed), 8)
    return {
        "hidden_in": draw_hidden_in(jax.random.fold_in(arg_keys[7], 71), 0),
        "lengths": uneven_parts(arg_keys[1], QUERIES, QUERIES * SEQ * 5 // 8, SEQ, 2).astype(jnp.int32),
        "gate_weight": centred(arg_keys[2], (D, FF), D ** -0.5, 0.09375, ((0, 4), (1, 8))),
        "up_weight": centred(arg_keys[3], (D, FF), D ** -0.5, 0.09375, ((0, 4), (1, 8))),
        "down_weight": draw_down_weight(jax.random.fold_in(arg_keys[7], 71), 0),
        "code_weight": draw_code_weight(jax.random.fold_in(arg_keys[7], 71), 0),
        "corpus_codes": draw_corpus_codes(jax.random.fold_in(arg_keys[7], 71), 0),
    }


epsilon = 1e-05

def keep_best(first, second):
    return lax.top_k(jnp.concatenate([first, second], axis=1), TOPK)[0]

def reference(hidden_in, lengths, gate_weight, up_weight, down_weight, code_weight, corpus_codes):
    widened = hidden_in.astype(jnp.float32)
    normed = (widened * lax.rsqrt(lax.optimization_barrier(jnp.mean(widened * widened, axis=1, keepdims=True)) + epsilon)).astype(jnp.bfloat16)
    gate_sum = jnp.dot(normed, gate_weight, preferred_element_type=jnp.float32)
    up_sum = jnp.dot(normed, up_weight, preferred_element_type=jnp.float32)
    hidden_units = (jax.nn.silu(gate_sum) * up_sum).astype(jnp.bfloat16)
    branch_out = jnp.dot(hidden_units, down_weight, preferred_element_type=jnp.float32)
    residual = widened + branch_out
    final_rows = residual * lax.rsqrt(lax.optimization_barrier(jnp.mean(residual * residual, axis=1, keepdims=True)) + epsilon)
    grouped = final_rows.reshape(QUERIES, SEQ, D)
    valid_mask = (jnp.arange(SEQ, dtype=jnp.int32)[None, :] < lengths[:, None]).astype(jnp.float32)
    pooled = lax.optimization_barrier(jnp.sum(grouped * valid_mask[:, :, None], axis=1)) / lengths[:, None].astype(jnp.float32)
    pooled = pooled.astype(jnp.bfloat16)
    query_codes = jnp.dot(pooled, code_weight, preferred_element_type=jnp.float32).astype(jnp.bfloat16)
    scale = 1.0 / math.sqrt(BITS)
    shards = corpus_codes.reshape(DOCS // DOCS_DEV, DOCS_DEV, BITS)

    def visit(carry, shard_codes):
        scores = lax.dot_general(query_codes, shard_codes, (((1,), (1,)), ((), ())), preferred_element_type=jnp.float32) * scale
        return (keep_best(carry, scores), None)
    start_best = jnp.full((QUERIES, TOPK), -1e+30, jnp.float32)
    top_scores, unused = lax.scan(visit, start_best, shards)
    return top_scores
```

```python
import functools
import math

import jax
import jax.numpy as jnp
from jax import lax
from jax.experimental import pallas as pl
from jax.experimental.pallas import tpu as pltpu
from jax.sharding import PartitionSpec as P

SEQ = 32
TOPK = 100
REAL_NUM, REAL_DEN = 5, 8
CHUNK = 256

epsilon = 1e-05
F32, BF16 = jnp.float32, jnp.bfloat16


def mm(a, b, precision=None):
    return lax.dot_general(a, b, (((1,), (0,)), ((), ())), precision=precision, preferred_element_type=F32)


def rcopy(src, dst, send, recv, dev):
    return pltpu.make_async_remote_copy(
        src_ref=src, dst_ref=dst, send_sem=send, recv_sem=recv,
        device_id=dev, device_id_type=pl.DeviceIdType.MESH)


def block_kernel(dims, hid, lens, gate_h, up_h, down_h, code_h, corp_h, out,
                 gate, up, down, code, corp, colbuf, lens_all, xall, psend, precv,
                 ss_send, ss_recv, hall, acc, lsend, lrecv, gsend, grecv, t_send, t_recv,
                 pp, prc, pblk, cpart, crecv, codes,
                 w_s, a_s, a_r, l_s, l_r, ch_s, ch_r, la_s, la_r, p_s, p_r, ss_s, ss_r, h_s, h_r,
                 lr_s, lr_r, g_s, g_r, t_s, t_r, pp_s, pp_r, pb_s, pb_r, c_s, c_r, o_s, o_r):
    nq, nc, r, nreal, tq, tb, nch, cw, d_all = dims
    q = lax.axis_index("query")
    c = lax.axis_index("corpus")
    g = c // r
    j = lax.rem(c, r)
    slots, w = hid.shape[0], hid.shape[1]
    total = nq * slots
    nqueries = total // SEQ
    bw = code.shape[1] // nq

    loads = []
    for i, (s, d) in enumerate(((gate_h, gate), (up_h, up), (down_h, down), (code_h, code), (corp_h, corp))):
        cp = pltpu.make_async_copy(s, d, w_s.at[i])
        cp.start()
        loads.append(cp)

    def rq(k):
        return lax.rem(q + k, nq)

    def rc(k):
        return lax.rem(c + k, nc)

    def lane(k):
        return lax.rem(j + k, r)

    barrier = pltpu.get_barrier_semaphore()
    for k in range(1, nq):
        pl.semaphore_signal(barrier, inc=1, device_id=(rq(k), c), device_id_type=pl.DeviceIdType.MESH)
    for k in range(1, nc):
        pl.semaphore_signal(barrier, inc=1, device_id=(q, rc(k)), device_id_type=pl.DeviceIdType.MESH)
    pl.semaphore_wait(barrier, nq - 1 + nc - 1)

    for k in range(1, nq):
        rcopy(lens, lens_all.at[q], l_s.at[k], l_r.at[q], (rq(k), c)).start()

    @pl.when(q != g)
    def _():
        rcopy(hid, colbuf.at[q], a_s, a_r.at[q], (g, c)).start()

    lens_all[q] = lens[...]
    for k in range(1, nq):
        s = rq(k)
        rcopy(lens, lens_all.at[s], l_s.at[k], l_r.at[s], (s, c)).wait_recv()
    lens_row = jnp.concatenate([lens_all[i] for i in range(nq)], axis=1)
    slot = lax.broadcasted_iota(jnp.int32, (8, total), 1)
    valid = lax.rem(slot, SEQ) < lens_row
    before = lax.broadcasted_iota(jnp.int32, (total, total), 0) < lax.broadcasted_iota(jnp.int32, (total, total), 1)
    pos = mm(valid.astype(F32).astype(BF16), before.astype(F32).astype(BF16)).astype(jnp.int32)
    pos = jnp.where(valid, pos, -1)[:1]

    def chunk(i, slot_j):
        return xall.at[slot_j, pl.ds(i * tq, tq)]

    def down_chain(i):
        return rcopy(chunk(i, j), chunk(i, j), ch_s.at[0, i], ch_r.at[i], (q, jnp.maximum(c - r, 0)))

    def up_chain(i):
        return rcopy(chunk(i, j), chunk(i, j), ch_s.at[1, i], ch_r.at[i], (q, jnp.minimum(c + r, nc - 1)))

    sends_up = jnp.logical_and(g >= q, g < nc // r - 1)
    sends_down = jnp.logical_and(g <= q, g > 0)

    @pl.when(q == g)
    def _():
        colbuf[q] = hid[...]
        for k in range(1, nq):
            s = rq(k)
            rcopy(hid, colbuf.at[s], a_s, a_r.at[s], (s, c)).wait_recv()
        stacked = colbuf[...].reshape(total, w)
        for i in range(nq):
            row = lax.broadcasted_iota(jnp.int32, (tq, total), 0) + i * tq
            pick = (pos == row).astype(F32).astype(BF16)
            xall[j, i * tq:(i + 1) * tq, :] = mm(pick, stacked).astype(BF16)

    for i in range(nq):
        @pl.when(q != g)
        def _(i=i):
            up_chain(i).wait_recv()

        @pl.when(sends_up)
        def _(i=i):
            up_chain(i).start()

        @pl.when(sends_down)
        def _(i=i):
            down_chain(i).start()

        for k in range(1, r):
            rcopy(chunk(i, j), chunk(i, j), la_s.at[k, i], la_r.at[j, i], (q, g * r + lane(k))).start()
    for i in range(nq):
        for k in range(1, r):
            s = lane(k)
            rcopy(chunk(i, s), chunk(i, s), la_s.at[k, i], la_r.at[s, i], (q, g * r + s)).wait_recv()

    loads[0].wait()
    loads[1].wait()

    sq = sum(jnp.sum(jnp.square(xall[i].astype(F32)), axis=1, keepdims=True) for i in range(r))
    for i in range(nq):
        ss_send[i] = jnp.broadcast_to(sq[i * tq:(i + 1) * tq], (tq, 128))
    for k in range(1, nq):
        d = rq(k)
        rcopy(ss_send.at[d], ss_recv.at[q], ss_s.at[k], ss_r.at[q], (d, c)).start()

    def part_send(n, k):
        d = rq(k)
        return rcopy(psend.at[n, d], precv.at[n, q], p_s.at[n, k], p_r.at[n, q], (d, c))

    def part_recv(n, k):
        s = rq(k)
        return rcopy(psend.at[n, s], precv.at[n, s], p_s.at[n, k], p_r.at[n, s], (s, c))

    def h_send(n, k):
        return rcopy(hall.at[n, q], hall.at[n, q], h_s.at[n, k], h_r.at[n, q], (rq(k), c))

    def h_recv(n, k):
        s = rq(k)
        return rcopy(hall.at[n, s], hall.at[n, s], h_s.at[n, k], h_r.at[n, s], (s, c))

    def matmuls(n, carry):
        cols = pl.ds(pl.multiple_of(n * cw, cw), cw)
        for e, wref in enumerate((gate, up)):
            full = sum(mm(xall[i], wref[i * w:(i + 1) * w, cols]) for i in range(r)).astype(BF16)
            for i in range(nq):
                psend[n, i, e] = full[i * tq:(i + 1) * tq]
        for k in range(1, nq):
            part_send(n, k).start()
        return carry

    lax.fori_loop(0, nch, matmuls, 0)

    ssum = ss_send[q]
    for k in range(1, nq):
        s = rq(k)
        rcopy(ss_send.at[s], ss_recv.at[s], ss_s.at[k], ss_r.at[s], (s, c)).wait_recv()
        ssum = ssum + ss_recv[s]
    inv = lax.rsqrt(ssum[:, :1] / d_all + epsilon)
    loads[2].wait()
    acc[...] = jnp.zeros_like(acc)

    def reduce_chunk(n):
        gsum = psend[n, q, 0].astype(F32)
        usum = psend[n, q, 1].astype(F32)
        for k in range(1, nq):
            part_recv(n, k).wait_recv()
            s = rq(k)
            gsum = gsum + precv[n, s, 0].astype(F32)
            usum = usum + precv[n, s, 1].astype(F32)
        gsum = gsum * inv
        usum = usum * inv
        hall[n, q] = (gsum / (1.0 + jnp.exp(-gsum)) * usum).astype(BF16)
        for k in range(1, nq):
            h_send(n, k).start()

    def down_chunk(n):
        for k in range(1, nq):
            h_recv(n, k).wait_recv()
        acc[...] += mm(hall[n].reshape(nreal, cw), down[pl.ds(pl.multiple_of(n * cw, cw), cw), :])

    reduce_chunk(0)

    def both(n, carry):
        reduce_chunk(n)
        down_chunk(n - 1)
        return carry

    lax.fori_loop(1, nch, both, 0)
    down_chunk(nch - 1)

    ng = nc // r
    for gg in range(ng):
        for jj in range(r):
            b = gg * r + jj
            lsend[jj, gg] = acc[b * tb:(b + 1) * tb].astype(BF16)
    for k in range(1, r):
        t = lane(k)
        rcopy(lsend.at[t], lrecv.at[j], lr_s.at[k], lr_r.at[j], (q, g * r + t)).start()
    mine = lsend[j].astype(F32)
    for k in range(1, r):
        s = lane(k)
        rcopy(lsend.at[s], lrecv.at[s], lr_s.at[k], lr_r.at[s], (q, g * r + s)).wait_recv()
        mine = mine + lrecv[s].astype(F32)
    gsend[...] = mine.astype(BF16)
    for k in range(1, ng):
        t = lax.rem(g + k, ng)
        rcopy(gsend.at[t], grecv.at[g], g_s.at[k], g_r.at[g], (q, t * r + j)).start()
    row = lax.broadcasted_iota(jnp.int32, (tb, nreal), 0) + c * tb
    own_rows = (lax.broadcasted_iota(jnp.int32, (tb, nreal), 1) == row).astype(F32).astype(BF16)
    residual = jnp.concatenate([mm(own_rows, xall[i]) for i in range(r)], axis=1)
    residual = residual + gsend[g].astype(F32)
    for k in range(1, ng):
        s = lax.rem(g + k, ng)
        rcopy(gsend.at[s], grecv.at[s], g_s.at[k], g_r.at[s], (q, s * r + j)).wait_recv()
        residual = residual + grecv[s].astype(F32)

    t_send[...] = jnp.broadcast_to(jnp.sum(residual * residual, axis=1, keepdims=True), (tb, 128))
    for k in range(1, nq):
        rcopy(t_send, t_recv.at[q], t_s.at[k], t_r.at[q], (rq(k), c)).start()
    qrow = lax.broadcasted_iota(jnp.int32, (nqueries, total), 0)
    qslot = lax.broadcasted_iota(jnp.int32, (nqueries, total), 1)
    lens_b = jnp.broadcast_to(lens_row[:1], (nqueries, total)).astype(F32)
    vals_b = jnp.broadcast_to(valid.astype(F32)[:1], (nqueries, total))
    len_col = jnp.sum(jnp.where(qslot == qrow * SEQ, lens_b, 0.0), axis=1, keepdims=True)
    off_col = jnp.sum(jnp.where(qslot < qrow * SEQ, vals_b, 0.0), axis=1, keepdims=True)
    prow = (lax.broadcasted_iota(jnp.int32, (nqueries, tb), 1) + c * tb).astype(F32)
    member = jnp.where(jnp.logical_and(prow >= off_col, prow < off_col + len_col), 1.0, 0.0)
    tsum = t_send[...]
    for k in range(1, nq):
        s = rq(k)
        rcopy(t_send, t_recv.at[s], t_s.at[k], t_r.at[s], (s, c)).wait_recv()
        tsum = tsum + t_recv[s]
    final = residual * lax.rsqrt(tsum[:, :1] / d_all + epsilon)
    pooled_part = mm(member, final, lax.Precision.HIGHEST)
    for i in range(r):
        pp[i] = pooled_part[:, i * w:(i + 1) * w]
    for i in range(r):
        @pl.when(c != q * r + i)
        def _(i=i):
            rcopy(pp.at[i], prc.at[c], pp_s.at[i], pp_r.at[c], (q, q * r + i)).start()

    @pl.when(g == q)
    def _():
        pooled = pp[j]
        for k in range(1, nc):
            s = rc(k)
            rcopy(pp.at[j], prc.at[s], pp_s.at[0], pp_r.at[s], (q, s)).wait_recv()
            pooled = pooled + prc[s]
        pblk[...] = (pooled / len_col).astype(BF16)
        for k in range(1, nq):
            rcopy(pblk, pblk, pb_s.at[k], pb_r, (rq(k), c)).start()

    loads[3].wait()
    loads[4].wait()

    @pl.when(g != q)
    def _():
        rcopy(pblk, pblk, pb_s.at[0], pb_r, (g, c)).wait_recv()

    cpart[...] = mm(pblk[...], code[:, pl.ds(pl.multiple_of(q * bw, bw), bw)])
    for k in range(1, nc):
        rcopy(cpart, crecv.at[c], c_s.at[k], c_r.at[c], (q, rc(k))).start()
    crecv[c] = cpart[...]
    for k in range(1, nc):
        s = rc(k)
        rcopy(cpart, crecv.at[s], c_s.at[k], c_r.at[s], (q, s)).wait_recv()
    csum = crecv[0]
    for i in range(1, nc):
        csum = csum + crecv[i]
    codes[q] = csum.astype(BF16)
    for k in range(1, nq):
        rcopy(codes.at[q], codes.at[q], o_s.at[k], o_r.at[q], (rq(k), c)).start()
    for k in range(1, nq):
        s = rq(k)
        rcopy(codes.at[s], codes.at[s], o_s.at[k], o_r.at[s], (s, c)).wait_recv()
    qcodes = jnp.concatenate([codes[i] for i in range(nq)], axis=1)
    scale = 1.0 / math.sqrt(corp.shape[1])
    out[...] = lax.dot_general(qcodes, corp[...], (((1,), (1,)), ((), ())), preferred_element_type=F32) * scale

    for k in range(1, nq):
        rcopy(lens, lens_all.at[q], l_s.at[k], l_r.at[q], (rq(k), c)).wait_send()
        rcopy(ss_send.at[q], ss_recv.at[q], ss_s.at[k], ss_r.at[q], (rq(k), c)).wait_send()
        rcopy(t_send, t_recv.at[q], t_s.at[k], t_r.at[q], (rq(k), c)).wait_send()
        rcopy(codes.at[q], codes.at[q], o_s.at[k], o_r.at[q], (rq(k), c)).wait_send()

    @pl.when(q != g)
    def _():
        rcopy(hid, colbuf.at[q], a_s, a_r.at[q], (g, c)).wait_send()

    for i in range(nq):
        @pl.when(sends_up)
        def _(i=i):
            up_chain(i).wait_send()

        @pl.when(sends_down)
        def _(i=i):
            down_chain(i).wait_send()

        for k in range(1, r):
            rcopy(chunk(i, j), chunk(i, j), la_s.at[k, i], la_r.at[j, i], (q, g * r + lane(k))).wait_send()

    def drain(n, carry):
        for k in range(1, nq):
            part_send(n, k).wait_send()
            h_send(n, k).wait_send()
        return carry

    lax.fori_loop(0, nch, drain, 0)
    for k in range(1, r):
        rcopy(lsend.at[lane(k)], lrecv.at[j], lr_s.at[k], lr_r.at[j], (q, g * r + lane(k))).wait_send()
    for k in range(1, ng):
        t = lax.rem(g + k, ng)
        rcopy(gsend.at[t], grecv.at[g], g_s.at[k], g_r.at[g], (q, t * r + j)).wait_send()
    for i in range(r):
        @pl.when(c != q * r + i)
        def _(i=i):
            rcopy(pp.at[i], prc.at[c], pp_s.at[i], pp_r.at[c], (q, q * r + i)).wait_send()

    @pl.when(g == q)
    def _():
        for k in range(1, nq):
            rcopy(pblk, pblk, pb_s.at[k], pb_r, (rq(k), c)).wait_send()
    for k in range(1, nc):
        rcopy(cpart, crecv.at[c], c_s.at[k], c_r.at[c], (q, rc(k))).wait_send()


def device_scores(nq, nc, hidden_in, lengths, gate_weight, up_weight, down_weight, code_weight, corpus_codes):
    slots, w = hidden_in.shape
    r = nc // nq
    nreal = nq * slots * REAL_NUM // REAL_DEN
    tq, tb = nreal // nq, nreal // nc
    dq, ffc = gate_weight.shape
    cw = CHUNK if ffc % CHUNK == 0 else ffc
    nch = ffc // cw
    nqueries = nq * lengths.shape[0]
    bits = code_weight.shape[1]
    bw = bits // nq
    ng = nc // r
    lens = jnp.broadcast_to(jnp.repeat(lengths, SEQ)[None, :], (8, slots))
    vm, dma = pltpu.VMEM, pltpu.SemaphoreType.DMA
    scratch = [
        vm(gate_weight.shape, BF16), vm(up_weight.shape, BF16), vm(down_weight.shape, BF16),
        vm(code_weight.shape, BF16), vm(corpus_codes.shape, BF16),
        vm((nq, slots, w), BF16), vm((nq, 8, slots), jnp.int32), vm((r, nreal, w), BF16),
        vm((nch, nq, 2, tq, cw), BF16), vm((nch, nq, 2, tq, cw), BF16),
        vm((nq, tq, 128), F32), vm((nq, tq, 128), F32), vm((nch, nq, tq, cw), BF16), vm((nreal, dq), F32),
        vm((r, ng, tb, dq), BF16), vm((r, ng, tb, dq), BF16), vm((ng, tb, dq), BF16), vm((ng, tb, dq), BF16),
        vm((tb, 128), F32), vm((nq, tb, 128), F32),
        vm((r, nqueries, w), F32), vm((nc, nqueries, w), F32), vm((nqueries, w), BF16),
        vm((nqueries, bw), F32), vm((nc, nqueries, bw), F32), vm((nq, nqueries, bw), BF16),
        dma((5,)), dma, dma((nq,)), dma((nq,)), dma((nq,)), dma((2, nq)), dma((nq,)), dma((r, nq)), dma((r, nq)),
        dma((nch, nq)), dma((nch, nq)), dma((nq,)), dma((nq,)), dma((nch, nq)), dma((nch, nq)),
        dma((r,)), dma((r,)), dma((ng,)), dma((ng,)), dma((nq,)), dma((nq,)),
        dma((r,)), dma((nc,)), dma((nq,)), dma, dma((nc,)), dma((nc,)), dma((nq,)), dma((nq,)),
    ]
    dims = (nq, nc, r, nreal, tq, tb, nch, cw, w * nc)
    vspec, aspec = pl.BlockSpec(memory_space=pltpu.VMEM), pl.BlockSpec(memory_space=pl.ANY)
    return pl.pallas_call(
        functools.partial(block_kernel, dims),
        out_shape=jax.ShapeDtypeStruct((nqueries, corpus_codes.shape[0]), F32),
        in_specs=[vspec, vspec] + [aspec] * 5,
        out_specs=vspec,
        scratch_shapes=scratch,
        compiler_params=pltpu.CompilerParams(
            collective_id=0, has_side_effects=True, vmem_limit_bytes=48 * 1024 * 1024),
    )(hidden_in, lens, gate_weight, up_weight, down_weight, code_weight, corpus_codes)


def per_device(nq, nc, *args):
    scores = device_scores(nq, nc, *args)
    local_best = lax.top_k(scores, min(TOPK, scores.shape[1]))[0]
    if nq * nc * local_best.shape[1] > 4096:
        local_best = lax.all_gather(local_best, "query", axis=1, tiled=True)
        local_best = lax.top_k(local_best, TOPK)[0]
        everyone = lax.all_gather(local_best, "corpus", axis=1, tiled=True)
    else:
        everyone = lax.all_gather(local_best, ("query", "corpus"), axis=1, tiled=True)
    return lax.top_k(everyone, TOPK)[0]


def solution(mesh):
    in_specs = (
        P("query", "corpus"),
        P("query"),
        P("query", "corpus"),
        P("query", "corpus"),
        P("corpus", "query"),
        P("corpus", None),
        P(("query", "corpus"), None),
    )
    body = functools.partial(per_device, mesh.shape["query"], mesh.shape["corpus"])
    return jax.shard_map(body, mesh=mesh, in_specs=in_specs, out_specs=P(), check_vma=False)
```

```python
import functools
import math

import jax
import jax.numpy as jnp
from jax import lax
from jax.experimental import pallas as pl
from jax.experimental.pallas import tpu as pltpu
from jax.sharding import PartitionSpec as P

SEQ = 32
LANES = 128
TOPK = 100
REAL_NUM, REAL_DEN = 5, 8
CHUNK = 256

epsilon = 1e-05
F32, BF16 = jnp.float32, jnp.bfloat16


def mm(a, b, precision=None):
    return lax.dot_general(a, b, (((1,), (0,)), ((), ())), precision=precision, preferred_element_type=F32)


def rcopy(src, dst, send, recv, dev):
    return pltpu.make_async_remote_copy(
        src_ref=src, dst_ref=dst, send_sem=send, recv_sem=recv,
        device_id=dev, device_id_type=pl.DeviceIdType.MESH)


def exchange(x, s, keep_max):
    bit = (lax.broadcasted_iota(jnp.int32, x.shape, 1) & s) != 0
    other = jnp.where(bit, pltpu.roll(x, s, 1), pltpu.roll(x, LANES - s, 1))
    return jnp.where(keep_max, jnp.maximum(x, other), jnp.minimum(x, other))


def sort_lanes(x):
    lane = lax.broadcasted_iota(jnp.int32, x.shape, 1)
    flip = (lax.broadcasted_iota(jnp.int32, x.shape, 0) >= x.shape[0] // 2).astype(jnp.int32)
    size = 2
    while size <= LANES:
        up = ((lane & size) != 0).astype(jnp.int32) if size < LANES else jnp.zeros_like(lane)
        s = size // 2
        while s:
            low = ((lane & s) != 0).astype(jnp.int32)
            x = exchange(x, s, (low ^ up ^ flip) == 0)
            s //= 2
        size *= 2
    return x


def merge_all(x, rows, lone):
    while x.shape[0] > rows:
        half = x.shape[0] // 2
        x = jnp.maximum(x[:half], x[half:])
        lane = lax.broadcasted_iota(jnp.int32, x.shape, 1)
        if half > rows:
            flip = (lax.broadcasted_iota(jnp.int32, x.shape, 0) >= half // 2).astype(jnp.int32)
        else:
            flip = jnp.zeros_like(lane) + jnp.asarray(lone, jnp.int32)
        s = LANES // 2
        while s:
            low = ((lane & s) != 0).astype(jnp.int32)
            x = exchange(x, s, (low ^ flip) == 0)
            s //= 2
    return x


def block_kernel(dims, hid, lens, gate_h, up_h, down_h, code_h, corp_h, out,
                 gate, up, down, code, corp, colbuf, lens_all, xall, psend, precv,
                 st_send, st_recv, inv_all, xn, pown, top_q, top_c, hall, acc, lsend, lrecv, gsend, grecv, t_send, t_recv,
                 pp, prc, pblk, cpart, crecv, codes,
                 w_s, a_s, a_r, l_s, l_r, ch_s, ch_r, la_s, la_r, p_s, p_r, st_s, st_r, iv_s, iv_r, tq_s, tq_r, tc_s, tc_r, h_s, h_r,
                 lr_s, lr_r, g_s, g_r, t_s, t_r, pp_s, pp_r, pb_s, pb_r, c_s, c_r, o_s, o_r):
    nq, nc, r, nreal, tq, tb, nch, cw, d_all = dims
    q = lax.axis_index("query")
    c = lax.axis_index("corpus")
    g = c // r
    j = lax.rem(c, r)
    slots, w = hid.shape[0], hid.shape[1]
    total = nq * slots
    nqueries = total // SEQ
    bw = code.shape[1] // nq

    loads = []
    for i, (s, d) in enumerate(((gate_h, gate), (up_h, up), (down_h, down), (code_h, code), (corp_h, corp))):
        cp = pltpu.make_async_copy(s, d, w_s.at[i])
        cp.start()
        loads.append(cp)

    def rq(k):
        return lax.rem(q + k, nq)

    def rc(k):
        return lax.rem(c + k, nc)

    def lane(k):
        return lax.rem(j + k, r)

    barrier = pltpu.get_barrier_semaphore()
    for k in range(1, nq):
        pl.semaphore_signal(barrier, inc=1, device_id=(rq(k), c), device_id_type=pl.DeviceIdType.MESH)
    for k in range(1, nc):
        pl.semaphore_signal(barrier, inc=1, device_id=(q, rc(k)), device_id_type=pl.DeviceIdType.MESH)
    pl.semaphore_wait(barrier, nq - 1 + nc - 1)

    for k in range(1, nq):
        rcopy(lens, lens_all.at[q], l_s.at[k], l_r.at[q], (rq(k), c)).start()

    @pl.when(q != g)
    def _():
        rcopy(hid, colbuf.at[q], a_s, a_r.at[q], (g, c)).start()

    squares = jnp.square(hid[...].astype(F32))
    st_send[...] = lax.dot_general(jnp.ones((8, w), F32), squares, (((1,), (1,)), ((), ())),
                                   precision=lax.Precision.HIGHEST, preferred_element_type=F32)
    for k in range(1, nc):
        rcopy(st_send, st_recv.at[c], st_s.at[k], st_r.at[c], (q, rc(k))).start()
    st_recv[c] = st_send[...]
    lens_all[q] = lens[...]
    for k in range(1, nq):
        s = rq(k)
        rcopy(lens, lens_all.at[s], l_s.at[k], l_r.at[s], (s, c)).wait_recv()
    lens_row = jnp.concatenate([lens_all[i] for i in range(nq)], axis=1)
    slot = lax.broadcasted_iota(jnp.int32, (8, total), 1)
    valid = lax.rem(slot, SEQ) < lens_row
    before = lax.broadcasted_iota(jnp.int32, (total, total), 0) < lax.broadcasted_iota(jnp.int32, (total, total), 1)
    pos = mm(valid.astype(F32).astype(BF16), before.astype(F32).astype(BF16)).astype(jnp.int32)
    pos = jnp.where(valid, pos, -1)[:1]

    for k in range(1, nc):
        s = rc(k)
        rcopy(st_send, st_recv.at[s], st_s.at[k], st_r.at[s], (q, s)).wait_recv()
    stat = st_recv[0]
    for i in range(1, nc):
        stat = stat + st_recv[i]
    inv_all[q] = lax.rsqrt(stat / d_all + epsilon)
    for k in range(1, nq):
        rcopy(inv_all.at[q], inv_all.at[q], iv_s.at[k], iv_r.at[q], (rq(k), c)).start()

    def chunk(i, slot_j):
        return xall.at[slot_j, pl.ds(i * tq, tq)]

    def down_chain(i):
        return rcopy(chunk(i, j), chunk(i, j), ch_s.at[0, i], ch_r.at[i], (q, jnp.maximum(c - r, 0)))

    def up_chain(i):
        return rcopy(chunk(i, j), chunk(i, j), ch_s.at[1, i], ch_r.at[i], (q, jnp.minimum(c + r, nc - 1)))

    sends_up = jnp.logical_and(g >= q, g < nc // r - 1)
    sends_down = jnp.logical_and(g <= q, g > 0)

    @pl.when(q == g)
    def _():
        colbuf[q] = hid[...]
        for k in range(1, nq):
            s = rq(k)
            rcopy(hid, colbuf.at[s], a_s, a_r.at[s], (s, c)).wait_recv()
        stacked = colbuf[...].reshape(total, w)
        for i in range(nq):
            row = lax.broadcasted_iota(jnp.int32, (tq, total), 0) + i * tq
            pick = (pos == row).astype(F32).astype(BF16)
            xall[j, i * tq:(i + 1) * tq, :] = mm(pick, stacked).astype(BF16)

    for i in range(nq):
        @pl.when(q != g)
        def _(i=i):
            up_chain(i).wait_recv()

        @pl.when(sends_up)
        def _(i=i):
            up_chain(i).start()

        @pl.when(sends_down)
        def _(i=i):
            down_chain(i).start()

        for k in range(1, r):
            rcopy(chunk(i, j), chunk(i, j), la_s.at[k, i], la_r.at[j, i], (q, g * r + lane(k))).start()
    for k in range(1, nq):
        s = rq(k)
        rcopy(inv_all.at[s], inv_all.at[s], iv_s.at[k], iv_r.at[s], (s, c)).wait_recv()
    inv_row = jnp.concatenate([inv_all[i] for i in range(nq)], axis=1)[:1]
    inv_cols = []
    for i in range(nq):
        row = lax.broadcasted_iota(jnp.int32, (tq, total), 0) + i * tq
        inv_cols.append(jnp.sum(jnp.where(pos == row, inv_row, 0.0), axis=1, keepdims=True))
    inv = jnp.concatenate(inv_cols, axis=0)
    for i in range(nq):
        for k in range(1, r):
            s = lane(k)
            rcopy(chunk(i, s), chunk(i, s), la_s.at[k, i], la_r.at[s, i], (q, g * r + s)).wait_recv()

    loads[0].wait()
    loads[1].wait()

    for i in range(r):
        xn[i] = (xall[i].astype(F32) * inv).astype(BF16)

    def part_send(n, k):
        d = rq(k)
        return rcopy(psend.at[n, d], precv.at[n, q], p_s.at[n, k], p_r.at[n, q], (d, c))

    def part_recv(n, k):
        s = rq(k)
        return rcopy(psend.at[n, s], precv.at[n, s], p_s.at[n, k], p_r.at[n, s], (s, c))

    def h_send(n, k):
        return rcopy(hall.at[n, q], hall.at[n, q], h_s.at[n, k], h_r.at[n, q], (rq(k), c))

    def h_recv(n, k):
        s = rq(k)
        return rcopy(hall.at[n, s], hall.at[n, s], h_s.at[n, k], h_r.at[n, s], (s, c))

    def matmuls(n, carry):
        cols = pl.ds(pl.multiple_of(n * cw, cw), cw)
        for e, wref in enumerate((gate, up)):
            full = sum(mm(xn[i], wref[i * w:(i + 1) * w, cols]) for i in range(r))
            for i in range(nq):
                psend[n, i, e] = full[i * tq:(i + 1) * tq].astype(BF16)

                @pl.when(q == i)
                def _(i=i, e=e, full=full):
                    pown[n, e] = full[i * tq:(i + 1) * tq]
        for k in range(1, nq):
            part_send(n, k).start()
        return carry

    lax.fori_loop(0, nch, matmuls, 0)

    loads[2].wait()
    acc[...] = jnp.zeros_like(acc)

    def reduce_chunk(n):
        gsum = pown[n, 0]
        usum = pown[n, 1]
        for k in range(1, nq):
            part_recv(n, k).wait_recv()
            s = rq(k)
            gsum = gsum + precv[n, s, 0].astype(F32)
            usum = usum + precv[n, s, 1].astype(F32)
        hall[n, q] = (gsum / (1.0 + jnp.exp(-gsum)) * usum).astype(BF16)
        for k in range(1, nq):
            h_send(n, k).start()

    def down_chunk(n):
        for k in range(1, nq):
            h_recv(n, k).wait_recv()
        acc[...] += mm(hall[n].reshape(nreal, cw), down[pl.ds(pl.multiple_of(n * cw, cw), cw), :])

    reduce_chunk(0)

    def both(n, carry):
        reduce_chunk(n)
        down_chunk(n - 1)
        return carry

    lax.fori_loop(1, nch, both, 0)
    down_chunk(nch - 1)

    ng = nc // r
    for gg in range(ng):
        for jj in range(r):
            b = gg * r + jj
            lsend[jj, gg] = acc[b * tb:(b + 1) * tb].astype(BF16)
    for k in range(1, r):
        t = lane(k)
        rcopy(lsend.at[t], lrecv.at[j], lr_s.at[k], lr_r.at[j], (q, g * r + t)).start()
    mine = lsend[j].astype(F32)
    for k in range(1, r):
        s = lane(k)
        rcopy(lsend.at[s], lrecv.at[s], lr_s.at[k], lr_r.at[s], (q, g * r + s)).wait_recv()
        mine = mine + lrecv[s].astype(F32)
    gsend[...] = mine.astype(BF16)
    for k in range(1, ng):
        t = lax.rem(g + k, ng)
        rcopy(gsend.at[t], grecv.at[g], g_s.at[k], g_r.at[g], (q, t * r + j)).start()
    row = lax.broadcasted_iota(jnp.int32, (tb, nreal), 0) + c * tb
    own_rows = (lax.broadcasted_iota(jnp.int32, (tb, nreal), 1) == row).astype(F32).astype(BF16)
    residual = jnp.concatenate([mm(own_rows, xall[i]) for i in range(r)], axis=1)
    residual = residual + gsend[g].astype(F32)
    for k in range(1, ng):
        s = lax.rem(g + k, ng)
        rcopy(gsend.at[s], grecv.at[s], g_s.at[k], g_r.at[s], (q, s * r + j)).wait_recv()
        residual = residual + grecv[s].astype(F32)

    t_send[...] = jnp.broadcast_to(jnp.sum(residual * residual, axis=1, keepdims=True), (tb, 128))
    for k in range(1, nq):
        rcopy(t_send, t_recv.at[q], t_s.at[k], t_r.at[q], (rq(k), c)).start()
    qrow = lax.broadcasted_iota(jnp.int32, (nqueries, total), 0)
    qslot = lax.broadcasted_iota(jnp.int32, (nqueries, total), 1)
    lens_b = jnp.broadcast_to(lens_row[:1], (nqueries, total)).astype(F32)
    vals_b = jnp.broadcast_to(valid.astype(F32)[:1], (nqueries, total))
    len_col = jnp.sum(jnp.where(qslot == qrow * SEQ, lens_b, 0.0), axis=1, keepdims=True)
    off_col = jnp.sum(jnp.where(qslot < qrow * SEQ, vals_b, 0.0), axis=1, keepdims=True)
    prow = (lax.broadcasted_iota(jnp.int32, (nqueries, tb), 1) + c * tb).astype(F32)
    member = jnp.where(jnp.logical_and(prow >= off_col, prow < off_col + len_col), 1.0, 0.0)
    tsum = t_send[...]
    for k in range(1, nq):
        s = rq(k)
        rcopy(t_send, t_recv.at[s], t_s.at[k], t_r.at[s], (s, c)).wait_recv()
        tsum = tsum + t_recv[s]
    final = residual * lax.rsqrt(tsum[:, :1] / d_all + epsilon)
    pooled_part = mm(member, final, lax.Precision.HIGHEST)
    for i in range(r):
        pp[i] = pooled_part[:, i * w:(i + 1) * w]
    for i in range(r):
        @pl.when(c != q * r + i)
        def _(i=i):
            rcopy(pp.at[i], prc.at[c], pp_s.at[i], pp_r.at[c], (q, q * r + i)).start()

    @pl.when(g == q)
    def _():
        pooled = pp[j]
        for k in range(1, nc):
            s = rc(k)
            rcopy(pp.at[j], prc.at[s], pp_s.at[0], pp_r.at[s], (q, s)).wait_recv()
            pooled = pooled + prc[s]
        pblk[...] = (pooled / len_col).astype(BF16)
        for k in range(1, nq):
            rcopy(pblk, pblk, pb_s.at[k], pb_r, (rq(k), c)).start()

    loads[3].wait()
    loads[4].wait()

    @pl.when(g != q)
    def _():
        rcopy(pblk, pblk, pb_s.at[0], pb_r, (g, c)).wait_recv()

    cpart[...] = mm(pblk[...], code[:, pl.ds(pl.multiple_of(q * bw, bw), bw)])
    for k in range(1, nc):
        rcopy(cpart, crecv.at[c], c_s.at[k], c_r.at[c], (q, rc(k))).start()
    crecv[c] = cpart[...]
    for k in range(1, nc):
        s = rc(k)
        rcopy(cpart, crecv.at[s], c_s.at[k], c_r.at[s], (q, s)).wait_recv()
    csum = crecv[0]
    for i in range(1, nc):
        csum = csum + crecv[i]
    codes[q] = csum.astype(BF16)
    for k in range(1, nq):
        rcopy(codes.at[q], codes.at[q], o_s.at[k], o_r.at[q], (rq(k), c)).start()
    for k in range(1, nq):
        s = rq(k)
        rcopy(codes.at[s], codes.at[s], o_s.at[k], o_r.at[s], (s, c)).wait_recv()
    qcodes = jnp.concatenate([codes[i] for i in range(nq)], axis=1)
    scale = 1.0 / math.sqrt(corp.shape[1])
    scores = lax.dot_general(qcodes, corp[...], (((1,), (1,)), ((), ())), preferred_element_type=F32) * scale

    blocks = corp.shape[0] // LANES
    lists = jnp.concatenate([scores[:, i * LANES:(i + 1) * LANES] for i in range(blocks)], axis=0)
    best = merge_all(sort_lanes(lists), nqueries, q >= nq // 2)
    top_q[q] = best
    for k in range(1, nq):
        rcopy(top_q.at[q], top_q.at[q], tq_s.at[k], tq_r.at[q], (rq(k), c)).start()
    for k in range(1, nq):
        s = rq(k)
        rcopy(top_q.at[s], top_q.at[s], tq_s.at[k], tq_r.at[s], (s, c)).wait_recv()
    best = merge_all(top_q[...].reshape(nq * nqueries, LANES), nqueries, c >= nc // 2)
    top_c[c] = best
    for k in range(1, nc):
        rcopy(top_c.at[c], top_c.at[c], tc_s.at[k], tc_r.at[c], (q, rc(k))).start()
    for k in range(1, nc):
        s = rc(k)
        rcopy(top_c.at[s], top_c.at[s], tc_s.at[k], tc_r.at[s], (q, s)).wait_recv()
    best = merge_all(top_c[...].reshape(nc * nqueries, LANES), nqueries, False)
    out[...] = best[:, :TOPK]

    for k in range(1, nq):
        rcopy(lens, lens_all.at[q], l_s.at[k], l_r.at[q], (rq(k), c)).wait_send()
        rcopy(inv_all.at[q], inv_all.at[q], iv_s.at[k], iv_r.at[q], (rq(k), c)).wait_send()
        rcopy(top_q.at[q], top_q.at[q], tq_s.at[k], tq_r.at[q], (rq(k), c)).wait_send()
        rcopy(t_send, t_recv.at[q], t_s.at[k], t_r.at[q], (rq(k), c)).wait_send()
        rcopy(codes.at[q], codes.at[q], o_s.at[k], o_r.at[q], (rq(k), c)).wait_send()

    @pl.when(q != g)
    def _():
        rcopy(hid, colbuf.at[q], a_s, a_r.at[q], (g, c)).wait_send()

    for i in range(nq):
        @pl.when(sends_up)
        def _(i=i):
            up_chain(i).wait_send()

        @pl.when(sends_down)
        def _(i=i):
            down_chain(i).wait_send()

        for k in range(1, r):
            rcopy(chunk(i, j), chunk(i, j), la_s.at[k, i], la_r.at[j, i], (q, g * r + lane(k))).wait_send()

    def drain(n, carry):
        for k in range(1, nq):
            part_send(n, k).wait_send()
            h_send(n, k).wait_send()
        return carry

    lax.fori_loop(0, nch, drain, 0)
    for k in range(1, r):
        rcopy(lsend.at[lane(k)], lrecv.at[j], lr_s.at[k], lr_r.at[j], (q, g * r + lane(k))).wait_send()
    for k in range(1, ng):
        t = lax.rem(g + k, ng)
        rcopy(gsend.at[t], grecv.at[g], g_s.at[k], g_r.at[g], (q, t * r + j)).wait_send()
    for i in range(r):
        @pl.when(c != q * r + i)
        def _(i=i):
            rcopy(pp.at[i], prc.at[c], pp_s.at[i], pp_r.at[c], (q, q * r + i)).wait_send()

    @pl.when(g == q)
    def _():
        for k in range(1, nq):
            rcopy(pblk, pblk, pb_s.at[k], pb_r, (rq(k), c)).wait_send()
    for k in range(1, nc):
        rcopy(cpart, crecv.at[c], c_s.at[k], c_r.at[c], (q, rc(k))).wait_send()
        rcopy(st_send, st_recv.at[c], st_s.at[k], st_r.at[c], (q, rc(k))).wait_send()
        rcopy(top_c.at[c], top_c.at[c], tc_s.at[k], tc_r.at[c], (q, rc(k))).wait_send()


def per_device(nq, nc, hidden_in, lengths, gate_weight, up_weight, down_weight, code_weight, corpus_codes):
    slots, w = hidden_in.shape
    r = nc // nq
    nreal = nq * slots * REAL_NUM // REAL_DEN
    tq, tb = nreal // nq, nreal // nc
    dq, ffc = gate_weight.shape
    cw = CHUNK if ffc % CHUNK == 0 else ffc
    nch = ffc // cw
    nqueries = nq * lengths.shape[0]
    bits = code_weight.shape[1]
    bw = bits // nq
    ng = nc // r
    lens = jnp.broadcast_to(jnp.repeat(lengths, SEQ)[None, :], (8, slots))
    vm, dma = pltpu.VMEM, pltpu.SemaphoreType.DMA
    scratch = [
        vm(gate_weight.shape, BF16), vm(up_weight.shape, BF16), vm(down_weight.shape, BF16),
        vm(code_weight.shape, BF16), vm(corpus_codes.shape, BF16),
        vm((nq, slots, w), BF16), vm((nq, 8, slots), jnp.int32), vm((r, nreal, w), BF16),
        vm((nch, nq, 2, tq, cw), BF16), vm((nch, nq, 2, tq, cw), BF16),
        vm((8, slots), F32), vm((nc, 8, slots), F32), vm((nq, 8, slots), F32), vm((r, nreal, w), BF16),
        vm((nch, 2, tq, cw), F32), vm((nq, nqueries, LANES), F32), vm((nc, nqueries, LANES), F32),
        vm((nch, nq, tq, cw), BF16), vm((nreal, dq), F32),
        vm((r, ng, tb, dq), BF16), vm((r, ng, tb, dq), BF16), vm((ng, tb, dq), BF16), vm((ng, tb, dq), BF16),
        vm((tb, 128), F32), vm((nq, tb, 128), F32),
        vm((r, nqueries, w), F32), vm((nc, nqueries, w), F32), vm((nqueries, w), BF16),
        vm((nqueries, bw), F32), vm((nc, nqueries, bw), F32), vm((nq, nqueries, bw), BF16),
        dma((5,)), dma, dma((nq,)), dma((nq,)), dma((nq,)), dma((2, nq)), dma((nq,)), dma((r, nq)), dma((r, nq)),
        dma((nch, nq)), dma((nch, nq)), dma((nc,)), dma((nc,)), dma((nq,)), dma((nq,)),
        dma((nq,)), dma((nq,)), dma((nc,)), dma((nc,)), dma((nch, nq)), dma((nch, nq)),
        dma((r,)), dma((r,)), dma((ng,)), dma((ng,)), dma((nq,)), dma((nq,)),
        dma((r,)), dma((nc,)), dma((nq,)), dma, dma((nc,)), dma((nc,)), dma((nq,)), dma((nq,)),
    ]
    dims = (nq, nc, r, nreal, tq, tb, nch, cw, w * nc)
    vspec, aspec = pl.BlockSpec(memory_space=pltpu.VMEM), pl.BlockSpec(memory_space=pl.ANY)
    return pl.pallas_call(
        functools.partial(block_kernel, dims),
        out_shape=jax.ShapeDtypeStruct((nqueries, TOPK), F32),
        in_specs=[vspec, vspec] + [aspec] * 5,
        out_specs=vspec,
        scratch_shapes=scratch,
        compiler_params=pltpu.CompilerParams(
            collective_id=0, has_side_effects=True, vmem_limit_bytes=60 * 1024 * 1024),
    )(hidden_in, lens, gate_weight, up_weight, down_weight, code_weight, corpus_codes)


def solution(mesh):
    in_specs = (
        P("query", "corpus"),
        P("query"),
        P("query", "corpus"),
        P("query", "corpus"),
        P("corpus", "query"),
        P("corpus", None),
        P(("query", "corpus"), None),
    )
    body = functools.partial(per_device, mesh.shape["query"], mesh.shape["corpus"])
    return jax.shard_map(body, mesh=mesh, in_specs=in_specs, out_specs=P(), check_vma=False)
```

```python
import functools
import math

import jax
import jax.numpy as jnp
from jax import lax
from jax.experimental import pallas as pl
from jax.experimental.pallas import tpu as pltpu
from jax.sharding import PartitionSpec as P

SEQ = 32
LANES = 128
TOPK = 100
REAL_NUM, REAL_DEN = 5, 8
CHUNK = 256

epsilon = 1e-05
F32, BF16 = jnp.float32, jnp.bfloat16


def mm(a, b, precision=None):
    return lax.dot_general(a, b, (((1,), (0,)), ((), ())), precision=precision, preferred_element_type=F32)


def rcopy(src, dst, send, recv, dev):
    return pltpu.make_async_remote_copy(
        src_ref=src, dst_ref=dst, send_sem=send, recv_sem=recv,
        device_id=dev, device_id_type=pl.DeviceIdType.MESH)


def exchange(x, s, keep_max):
    bit = (lax.broadcasted_iota(jnp.int32, x.shape, 1) & s) != 0
    other = jnp.where(bit, pltpu.roll(x, s, 1), pltpu.roll(x, LANES - s, 1))
    return jnp.where(keep_max, jnp.maximum(x, other), jnp.minimum(x, other))


def sort_lanes(x):
    lane = lax.broadcasted_iota(jnp.int32, x.shape, 1)
    flip = (lax.broadcasted_iota(jnp.int32, x.shape, 0) >= x.shape[0] // 2).astype(jnp.int32)
    size = 2
    while size <= LANES:
        up = ((lane & size) != 0).astype(jnp.int32) if size < LANES else jnp.zeros_like(lane)
        s = size // 2
        while s:
            low = ((lane & s) != 0).astype(jnp.int32)
            x = exchange(x, s, (low ^ up ^ flip) == 0)
            s //= 2
        size *= 2
    return x


def merge_all(x, rows, lone):
    while x.shape[0] > rows:
        half = x.shape[0] // 2
        x = jnp.maximum(x[:half], x[half:])
        lane = lax.broadcasted_iota(jnp.int32, x.shape, 1)
        if half > rows:
            flip = (lax.broadcasted_iota(jnp.int32, x.shape, 0) >= half // 2).astype(jnp.int32)
        else:
            flip = jnp.zeros_like(lane) + jnp.asarray(lone, jnp.int32)
        s = LANES // 2
        while s:
            low = ((lane & s) != 0).astype(jnp.int32)
            x = exchange(x, s, (low ^ flip) == 0)
            s //= 2
    return x


def block_kernel(dims, hid, lens, gate_h, up_h, down_h, code_h, corp_h, out,
                 gate, up, down, code, corp, colbuf, lens_all, xall, psend, precv,
                 st_send, st_recv, inv_all, xn, pown, top_q, top_c, hall, acc, lsend, lrecv, gsend, grecv, t_send, t_recv,
                 pp, prc, pblk, cpart, crecv, codes,
                 w_s, a_s, a_r, l_s, l_r, ch_s, ch_r, la_s, la_r, p_s, p_r, st_s, st_r, iv_s, iv_r, tq_s, tq_r, tc_s, tc_r, h_s, h_r,
                 lr_s, lr_r, g_s, g_r, t_s, t_r, pp_s, pp_r, pb_s, pb_r, c_s, c_r, o_s, o_r):
    nq, nc, r, nreal, tq, tb, nch, cw, d_all = dims
    q = lax.axis_index("query")
    c = lax.axis_index("corpus")
    g = c // r
    j = lax.rem(c, r)
    slots, w = hid.shape[0], hid.shape[1]
    total = nq * slots
    nqueries = total // SEQ
    bw = code.shape[1] // nq

    loads = []
    for i, (s, d) in enumerate(((gate_h, gate), (up_h, up), (down_h, down), (code_h, code), (corp_h, corp))):
        cp = pltpu.make_async_copy(s, d, w_s.at[i])
        cp.start()
        loads.append(cp)

    def rq(k):
        return lax.rem(q + k, nq)

    def rc(k):
        return lax.rem(c + k, nc)

    def lane(k):
        return lax.rem(j + k, r)

    barrier = pltpu.get_barrier_semaphore()
    for k in range(1, nq):
        pl.semaphore_signal(barrier, inc=1, device_id=(rq(k), c), device_id_type=pl.DeviceIdType.MESH)
    for k in range(1, nc):
        pl.semaphore_signal(barrier, inc=1, device_id=(q, rc(k)), device_id_type=pl.DeviceIdType.MESH)
    pl.semaphore_wait(barrier, nq - 1 + nc - 1)

    for k in range(1, nq):
        rcopy(lens, lens_all.at[q], l_s.at[k], l_r.at[q], (rq(k), c)).start()

    @pl.when(q != g)
    def _():
        rcopy(hid, colbuf.at[q], a_s, a_r.at[q], (g, c)).start()

    squares = jnp.square(hid[...].astype(F32))
    st_send[...] = lax.dot_general(jnp.ones((8, w), F32), squares, (((1,), (1,)), ((), ())),
                                   precision=lax.Precision.HIGHEST, preferred_element_type=F32)
    for k in range(1, nc):
        rcopy(st_send, st_recv.at[c], st_s.at[k], st_r.at[c], (q, rc(k))).start()
    st_recv[c] = st_send[...]
    lens_all[q] = lens[...]
    for k in range(1, nq):
        s = rq(k)
        rcopy(lens, lens_all.at[s], l_s.at[k], l_r.at[s], (s, c)).wait_recv()
    lens_row = jnp.concatenate([lens_all[i] for i in range(nq)], axis=1)
    slot = lax.broadcasted_iota(jnp.int32, (8, total), 1)
    valid = lax.rem(slot, SEQ) < lens_row
    before = lax.broadcasted_iota(jnp.int32, (total, total), 0) < lax.broadcasted_iota(jnp.int32, (total, total), 1)
    pos = mm(valid.astype(F32).astype(BF16), before.astype(F32).astype(BF16)).astype(jnp.int32)
    pos = jnp.where(valid, pos, -1)[:1]

    for k in range(1, nc):
        s = rc(k)
        rcopy(st_send, st_recv.at[s], st_s.at[k], st_r.at[s], (q, s)).wait_recv()
    stat = st_recv[0]
    for i in range(1, nc):
        stat = stat + st_recv[i]
    inv_all[q] = lax.rsqrt(stat / d_all + epsilon)
    for k in range(1, nq):
        rcopy(inv_all.at[q], inv_all.at[q], iv_s.at[k], iv_r.at[q], (rq(k), c)).start()

    def chunk(i, slot_j):
        return xall.at[slot_j, pl.ds(i * tq, tq)]

    def down_chain(i):
        return rcopy(chunk(i, j), chunk(i, j), ch_s.at[0, i], ch_r.at[i], (q, jnp.maximum(c - r, 0)))

    def up_chain(i):
        return rcopy(chunk(i, j), chunk(i, j), ch_s.at[1, i], ch_r.at[i], (q, jnp.minimum(c + r, nc - 1)))

    sends_up = jnp.logical_and(g >= q, g < nc // r - 1)
    sends_down = jnp.logical_and(g <= q, g > 0)

    @pl.when(q == g)
    def _():
        colbuf[q] = hid[...]
        for k in range(1, nq):
            s = rq(k)
            rcopy(hid, colbuf.at[s], a_s, a_r.at[s], (s, c)).wait_recv()
        stacked = colbuf[...].reshape(total, w)
        for i in range(nq):
            row = lax.broadcasted_iota(jnp.int32, (tq, total), 0) + i * tq
            pick = (pos == row).astype(F32).astype(BF16)
            xall[j, i * tq:(i + 1) * tq, :] = mm(pick, stacked).astype(BF16)

    for i in range(nq):
        @pl.when(q != g)
        def _(i=i):
            up_chain(i).wait_recv()

        @pl.when(sends_up)
        def _(i=i):
            up_chain(i).start()

        @pl.when(sends_down)
        def _(i=i):
            down_chain(i).start()

        for k in range(1, r):
            rcopy(chunk(i, j), chunk(i, j), la_s.at[k, i], la_r.at[j, i], (q, g * r + lane(k))).start()
    for k in range(1, nq):
        s = rq(k)
        rcopy(inv_all.at[s], inv_all.at[s], iv_s.at[k], iv_r.at[s], (s, c)).wait_recv()
    inv_row = jnp.concatenate([inv_all[i] for i in range(nq)], axis=1)[:1]
    inv_cols = []
    for i in range(nq):
        row = lax.broadcasted_iota(jnp.int32, (tq, total), 0) + i * tq
        inv_cols.append(jnp.sum(jnp.where(pos == row, inv_row, 0.0), axis=1, keepdims=True))
    inv = jnp.concatenate(inv_cols, axis=0)
    for i in range(nq):
        for k in range(1, r):
            s = lane(k)
            rcopy(chunk(i, s), chunk(i, s), la_s.at[k, i], la_r.at[s, i], (q, g * r + s)).wait_recv()

    loads[0].wait()
    loads[1].wait()

    for i in range(r):
        xn[i] = (xall[i].astype(F32) * inv).astype(BF16)

    side_a = q + 1 - 2 * lax.rem(q, 2)
    side_b = q + 2 - 4 * (q // 2)
    far = nq - 1 - q

    def sides(n):
        odd = lax.rem(n, 2)
        return side_a + (side_b - side_a) * odd, side_b + (side_a - side_b) * odd

    def near_part(n):
        one, _ = sides(n)
        return rcopy(psend.at[n, one], precv.at[n, 0], p_s.at[n, 0], p_r.at[n, 0], (one, c))

    def far_part(n):
        one, _ = sides(n)
        return rcopy(psend.at[n, far], precv.at[n, 1], p_s.at[n, 1], p_r.at[n, 1], (one, c))

    def passed_part(n):
        _, two = sides(n)
        return rcopy(precv.at[n, 3], precv.at[n, 2], p_s.at[n, 2], p_r.at[n, 2], (two, c))

    def h_near(n, k):
        to = sides(n)[k]
        return rcopy(hall.at[n, q], hall.at[n, q], h_s.at[n, k], h_r.at[n, k], (to, c))

    def h_near_in(n, k):
        to = sides(n)[k]
        return rcopy(hall.at[n, to], hall.at[n, to], h_s.at[n, k], h_r.at[n, k], (to, c))

    def h_pass(n):
        one, two = sides(n)
        return rcopy(hall.at[n, one], hall.at[n, one], h_s.at[n, 2], h_r.at[n, 2], (two, c))

    def h_pass_in(n):
        _, two = sides(n)
        return rcopy(hall.at[n, far], hall.at[n, far], h_s.at[n, 2], h_r.at[n, 2], (two, c))

    def matmuls(n, carry):
        cols = pl.ds(pl.multiple_of(n * cw, cw), cw)
        for e, wref in enumerate((gate, up)):
            full = sum(mm(xn[i], wref[i * w:(i + 1) * w, cols]) for i in range(r))
            for i in range(nq):
                psend[n, i, e] = full[i * tq:(i + 1) * tq].astype(BF16)

                @pl.when(q == i)
                def _(i=i, e=e, full=full):
                    pown[n, e] = full[i * tq:(i + 1) * tq]
        far_part(n).start()
        near_part(n).start()
        return carry

    lax.fori_loop(0, nch, matmuls, 0)

    loads[2].wait()
    acc[...] = jnp.zeros_like(acc)

    def pass_chunk(n):
        _, two = sides(n)
        far_part(n).wait_recv()
        precv[n, 3] = (psend[n, two].astype(F32) + precv[n, 1].astype(F32)).astype(BF16)
        passed_part(n).start()

    def reduce_chunk(n):
        near_part(n).wait_recv()
        passed_part(n).wait_recv()
        gsum = pown[n, 0] + precv[n, 0, 0].astype(F32) + precv[n, 2, 0].astype(F32)
        usum = pown[n, 1] + precv[n, 0, 1].astype(F32) + precv[n, 2, 1].astype(F32)
        hall[n, q] = (gsum / (1.0 + jnp.exp(-gsum)) * usum).astype(BF16)
        h_near(n, 0).start()
        h_near(n, 1).start()

    def relay_chunk(n):
        h_near_in(n, 0).wait_recv()
        h_pass(n).start()

    def down_chunk(n):
        h_near_in(n, 1).wait_recv()
        h_pass_in(n).wait_recv()
        acc[...] += mm(hall[n].reshape(nreal, cw), down[pl.ds(pl.multiple_of(n * cw, cw), cw), :])

    def passes(n, carry):
        pass_chunk(n)
        return carry

    lax.fori_loop(0, nch, passes, 0)
    reduce_chunk(0)

    def reduces(n, carry):
        reduce_chunk(n)
        relay_chunk(n - 1)
        return carry

    lax.fori_loop(1, nch, reduces, 0)
    relay_chunk(nch - 1)

    def downs(n, carry):
        down_chunk(n)
        return carry

    lax.fori_loop(0, nch, downs, 0)

    ng = nc // r
    for gg in range(ng):
        for jj in range(r):
            b = gg * r + jj
            lsend[jj, gg] = acc[b * tb:(b + 1) * tb].astype(BF16)
    for k in range(1, r):
        t = lane(k)
        rcopy(lsend.at[t], lrecv.at[j], lr_s.at[k], lr_r.at[j], (q, g * r + t)).start()
    mine = lsend[j].astype(F32)
    for k in range(1, r):
        s = lane(k)
        rcopy(lsend.at[s], lrecv.at[s], lr_s.at[k], lr_r.at[s], (q, g * r + s)).wait_recv()
        mine = mine + lrecv[s].astype(F32)
    gsend[...] = mine.astype(BF16)
    for k in range(1, ng):
        t = lax.rem(g + k, ng)
        rcopy(gsend.at[t], grecv.at[g], g_s.at[k], g_r.at[g], (q, t * r + j)).start()
    row = lax.broadcasted_iota(jnp.int32, (tb, nreal), 0) + c * tb
    own_rows = (lax.broadcasted_iota(jnp.int32, (tb, nreal), 1) == row).astype(F32).astype(BF16)
    residual = jnp.concatenate([mm(own_rows, xall[i]) for i in range(r)], axis=1)
    residual = residual + gsend[g].astype(F32)
    for k in range(1, ng):
        s = lax.rem(g + k, ng)
        rcopy(gsend.at[s], grecv.at[s], g_s.at[k], g_r.at[s], (q, s * r + j)).wait_recv()
        residual = residual + grecv[s].astype(F32)

    t_send[...] = jnp.broadcast_to(jnp.sum(residual * residual, axis=1, keepdims=True), (tb, 128))
    for k in range(1, nq):
        rcopy(t_send, t_recv.at[q], t_s.at[k], t_r.at[q], (rq(k), c)).start()
    qrow = lax.broadcasted_iota(jnp.int32, (nqueries, total), 0)
    qslot = lax.broadcasted_iota(jnp.int32, (nqueries, total), 1)
    lens_b = jnp.broadcast_to(lens_row[:1], (nqueries, total)).astype(F32)
    vals_b = jnp.broadcast_to(valid.astype(F32)[:1], (nqueries, total))
    len_col = jnp.sum(jnp.where(qslot == qrow * SEQ, lens_b, 0.0), axis=1, keepdims=True)
    off_col = jnp.sum(jnp.where(qslot < qrow * SEQ, vals_b, 0.0), axis=1, keepdims=True)
    prow = (lax.broadcasted_iota(jnp.int32, (nqueries, tb), 1) + c * tb).astype(F32)
    member = jnp.where(jnp.logical_and(prow >= off_col, prow < off_col + len_col), 1.0, 0.0)
    tsum = t_send[...]
    for k in range(1, nq):
        s = rq(k)
        rcopy(t_send, t_recv.at[s], t_s.at[k], t_r.at[s], (s, c)).wait_recv()
        tsum = tsum + t_recv[s]
    final = residual * lax.rsqrt(tsum[:, :1] / d_all + epsilon)
    pooled_part = mm(member, final, lax.Precision.HIGHEST)
    for i in range(r):
        pp[i] = pooled_part[:, i * w:(i + 1) * w]
    for i in range(r):
        @pl.when(c != q * r + i)
        def _(i=i):
            rcopy(pp.at[i], prc.at[c], pp_s.at[i], pp_r.at[c], (q, q * r + i)).start()

    @pl.when(g == q)
    def _():
        pooled = pp[j]
        for k in range(1, nc):
            s = rc(k)
            rcopy(pp.at[j], prc.at[s], pp_s.at[0], pp_r.at[s], (q, s)).wait_recv()
            pooled = pooled + prc[s]
        pblk[...] = (pooled / len_col).astype(BF16)
        for k in range(1, nq):
            rcopy(pblk, pblk, pb_s.at[k], pb_r, (rq(k), c)).start()

    loads[3].wait()
    loads[4].wait()

    @pl.when(g != q)
    def _():
        rcopy(pblk, pblk, pb_s.at[0], pb_r, (g, c)).wait_recv()

    cpart[...] = mm(pblk[...], code[:, pl.ds(pl.multiple_of(q * bw, bw), bw)])
    for k in range(1, nc):
        rcopy(cpart, crecv.at[c], c_s.at[k], c_r.at[c], (q, rc(k))).start()
    crecv[c] = cpart[...]
    for k in range(1, nc):
        s = rc(k)
        rcopy(cpart, crecv.at[s], c_s.at[k], c_r.at[s], (q, s)).wait_recv()
    csum = crecv[0]
    for i in range(1, nc):
        csum = csum + crecv[i]
    codes[q] = csum.astype(BF16)
    for k in range(1, nq):
        rcopy(codes.at[q], codes.at[q], o_s.at[k], o_r.at[q], (rq(k), c)).start()
    for k in range(1, nq):
        s = rq(k)
        rcopy(codes.at[s], codes.at[s], o_s.at[k], o_r.at[s], (s, c)).wait_recv()
    qcodes = jnp.concatenate([codes[i] for i in range(nq)], axis=1)
    scale = 1.0 / math.sqrt(corp.shape[1])
    scores = lax.dot_general(qcodes, corp[...], (((1,), (1,)), ((), ())), preferred_element_type=F32) * scale

    blocks = corp.shape[0] // LANES
    lists = jnp.concatenate([scores[:, i * LANES:(i + 1) * LANES] for i in range(blocks)], axis=0)
    best = merge_all(sort_lanes(lists), nqueries, q >= nq // 2)
    top_q[q] = best
    for k in range(1, nq):
        rcopy(top_q.at[q], top_q.at[q], tq_s.at[k], tq_r.at[q], (rq(k), c)).start()
    for k in range(1, nq):
        s = rq(k)
        rcopy(top_q.at[s], top_q.at[s], tq_s.at[k], tq_r.at[s], (s, c)).wait_recv()
    best = merge_all(top_q[...].reshape(nq * nqueries, LANES), nqueries, c >= nc // 2)
    top_c[c] = best
    for k in range(1, nc):
        rcopy(top_c.at[c], top_c.at[c], tc_s.at[k], tc_r.at[c], (q, rc(k))).start()
    for k in range(1, nc):
        s = rc(k)
        rcopy(top_c.at[s], top_c.at[s], tc_s.at[k], tc_r.at[s], (q, s)).wait_recv()
    best = merge_all(top_c[...].reshape(nc * nqueries, LANES), nqueries, False)
    out[...] = best[:, :TOPK]

    for k in range(1, nq):
        rcopy(lens, lens_all.at[q], l_s.at[k], l_r.at[q], (rq(k), c)).wait_send()
        rcopy(inv_all.at[q], inv_all.at[q], iv_s.at[k], iv_r.at[q], (rq(k), c)).wait_send()
        rcopy(top_q.at[q], top_q.at[q], tq_s.at[k], tq_r.at[q], (rq(k), c)).wait_send()
        rcopy(t_send, t_recv.at[q], t_s.at[k], t_r.at[q], (rq(k), c)).wait_send()
        rcopy(codes.at[q], codes.at[q], o_s.at[k], o_r.at[q], (rq(k), c)).wait_send()

    @pl.when(q != g)
    def _():
        rcopy(hid, colbuf.at[q], a_s, a_r.at[q], (g, c)).wait_send()

    for i in range(nq):
        @pl.when(sends_up)
        def _(i=i):
            up_chain(i).wait_send()

        @pl.when(sends_down)
        def _(i=i):
            down_chain(i).wait_send()

        for k in range(1, r):
            rcopy(chunk(i, j), chunk(i, j), la_s.at[k, i], la_r.at[j, i], (q, g * r + lane(k))).wait_send()

    def drain(n, carry):
        far_part(n).wait_send()
        near_part(n).wait_send()
        passed_part(n).wait_send()
        h_near(n, 0).wait_send()
        h_near(n, 1).wait_send()
        h_pass(n).wait_send()
        return carry

    lax.fori_loop(0, nch, drain, 0)
    for k in range(1, r):
        rcopy(lsend.at[lane(k)], lrecv.at[j], lr_s.at[k], lr_r.at[j], (q, g * r + lane(k))).wait_send()
    for k in range(1, ng):
        t = lax.rem(g + k, ng)
        rcopy(gsend.at[t], grecv.at[g], g_s.at[k], g_r.at[g], (q, t * r + j)).wait_send()
    for i in range(r):
        @pl.when(c != q * r + i)
        def _(i=i):
            rcopy(pp.at[i], prc.at[c], pp_s.at[i], pp_r.at[c], (q, q * r + i)).wait_send()

    @pl.when(g == q)
    def _():
        for k in range(1, nq):
            rcopy(pblk, pblk, pb_s.at[k], pb_r, (rq(k), c)).wait_send()
    for k in range(1, nc):
        rcopy(cpart, crecv.at[c], c_s.at[k], c_r.at[c], (q, rc(k))).wait_send()
        rcopy(st_send, st_recv.at[c], st_s.at[k], st_r.at[c], (q, rc(k))).wait_send()
        rcopy(top_c.at[c], top_c.at[c], tc_s.at[k], tc_r.at[c], (q, rc(k))).wait_send()


def per_device(nq, nc, hidden_in, lengths, gate_weight, up_weight, down_weight, code_weight, corpus_codes):
    slots, w = hidden_in.shape
    r = nc // nq
    nreal = nq * slots * REAL_NUM // REAL_DEN
    tq, tb = nreal // nq, nreal // nc
    dq, ffc = gate_weight.shape
    cw = CHUNK if ffc % CHUNK == 0 else ffc
    nch = ffc // cw
    nqueries = nq * lengths.shape[0]
    bits = code_weight.shape[1]
    bw = bits // nq
    ng = nc // r
    lens = jnp.broadcast_to(jnp.repeat(lengths, SEQ)[None, :], (8, slots))
    vm, dma = pltpu.VMEM, pltpu.SemaphoreType.DMA
    scratch = [
        vm(gate_weight.shape, BF16), vm(up_weight.shape, BF16), vm(down_weight.shape, BF16),
        vm(code_weight.shape, BF16), vm(corpus_codes.shape, BF16),
        vm((nq, slots, w), BF16), vm((nq, 8, slots), jnp.int32), vm((r, nreal, w), BF16),
        vm((nch, nq, 2, tq, cw), BF16), vm((nch, nq, 2, tq, cw), BF16),
        vm((8, slots), F32), vm((nc, 8, slots), F32), vm((nq, 8, slots), F32), vm((r, nreal, w), BF16),
        vm((nch, 2, tq, cw), F32), vm((nq, nqueries, LANES), F32), vm((nc, nqueries, LANES), F32),
        vm((nch, nq, tq, cw), BF16), vm((nreal, dq), F32),
        vm((r, ng, tb, dq), BF16), vm((r, ng, tb, dq), BF16), vm((ng, tb, dq), BF16), vm((ng, tb, dq), BF16),
        vm((tb, 128), F32), vm((nq, tb, 128), F32),
        vm((r, nqueries, w), F32), vm((nc, nqueries, w), F32), vm((nqueries, w), BF16),
        vm((nqueries, bw), F32), vm((nc, nqueries, bw), F32), vm((nq, nqueries, bw), BF16),
        dma((5,)), dma, dma((nq,)), dma((nq,)), dma((nq,)), dma((2, nq)), dma((nq,)), dma((r, nq)), dma((r, nq)),
        dma((nch, nq)), dma((nch, nq)), dma((nc,)), dma((nc,)), dma((nq,)), dma((nq,)),
        dma((nq,)), dma((nq,)), dma((nc,)), dma((nc,)), dma((nch, nq)), dma((nch, nq)),
        dma((r,)), dma((r,)), dma((ng,)), dma((ng,)), dma((nq,)), dma((nq,)),
        dma((r,)), dma((nc,)), dma((nq,)), dma, dma((nc,)), dma((nc,)), dma((nq,)), dma((nq,)),
    ]
    dims = (nq, nc, r, nreal, tq, tb, nch, cw, w * nc)
    vspec, aspec = pl.BlockSpec(memory_space=pltpu.VMEM), pl.BlockSpec(memory_space=pl.ANY)
    return pl.pallas_call(
        functools.partial(block_kernel, dims),
        out_shape=jax.ShapeDtypeStruct((nqueries, TOPK), F32),
        in_specs=[vspec, vspec] + [aspec] * 5,
        out_specs=vspec,
        scratch_shapes=scratch,
        compiler_params=pltpu.CompilerParams(
            collective_id=0, has_side_effects=True, vmem_limit_bytes=60 * 1024 * 1024),
    )(hidden_in, lens, gate_weight, up_weight, down_weight, code_weight, corpus_codes)


def solution(mesh):
    in_specs = (
        P("query", "corpus"),
        P("query"),
        P("query", "corpus"),
        P("query", "corpus"),
        P("corpus", "query"),
        P("corpus", None),
        P(("query", "corpus"), None),
    )
    body = functools.partial(per_device, mesh.shape["query"], mesh.shape["corpus"])
    return jax.shard_map(body, mesh=mesh, in_specs=in_specs, out_specs=P(), check_vma=False)
```

```python
import functools
import math

import jax
import jax.numpy as jnp
from jax import lax
from jax.experimental import pallas as pl
from jax.experimental.pallas import tpu as pltpu
from jax.sharding import PartitionSpec as P

SEQ = 32
LANES = 128
TOPK = 100
REAL_NUM, REAL_DEN = 5, 8
CHUNK = 256
PIECE = 32

epsilon = 1e-05
F32, BF16 = jnp.float32, jnp.bfloat16


def mm(a, b, precision=None):
    return lax.dot_general(a, b, (((1,), (0,)), ((), ())), precision=precision, preferred_element_type=F32)


def rcopy(src, dst, send, recv, dev):
    return pltpu.make_async_remote_copy(
        src_ref=src, dst_ref=dst, send_sem=send, recv_sem=recv,
        device_id=dev, device_id_type=pl.DeviceIdType.MESH)


def exchange(x, s, keep_max):
    bit = (lax.broadcasted_iota(jnp.int32, x.shape, 1) & s) != 0
    other = jnp.where(bit, pltpu.roll(x, s, 1), pltpu.roll(x, LANES - s, 1))
    return jnp.where(keep_max, jnp.maximum(x, other), jnp.minimum(x, other))


def sort_lanes(x):
    lane = lax.broadcasted_iota(jnp.int32, x.shape, 1)
    flip = (lax.broadcasted_iota(jnp.int32, x.shape, 0) >= x.shape[0] // 2).astype(jnp.int32)
    size = 2
    while size <= LANES:
        up = ((lane & size) != 0).astype(jnp.int32) if size < LANES else jnp.zeros_like(lane)
        s = size // 2
        while s:
            low = ((lane & s) != 0).astype(jnp.int32)
            x = exchange(x, s, (low ^ up ^ flip) == 0)
            s //= 2
        size *= 2
    return x


def merge_all(x, rows, lone):
    while x.shape[0] > rows:
        half = x.shape[0] // 2
        x = jnp.maximum(x[:half], x[half:])
        lane = lax.broadcasted_iota(jnp.int32, x.shape, 1)
        if half > rows:
            flip = (lax.broadcasted_iota(jnp.int32, x.shape, 0) >= half // 2).astype(jnp.int32)
        else:
            flip = jnp.zeros_like(lane) + jnp.asarray(lone, jnp.int32)
        s = LANES // 2
        while s:
            low = ((lane & s) != 0).astype(jnp.int32)
            x = exchange(x, s, (low ^ flip) == 0)
            s //= 2
    return x


def block_kernel(dims, hid, lens, gate_h, up_h, down_h, code_h, corp_h, out,
                 gate, up, down, code, corp, colbuf, lens_all, xall, psend, precv,
                 st_send, st_recv, inv_all, xn, pown, top_q, top_c, hall, acc, lsend, lrecv, gsend, grecv, t_send, t_recv,
                 pp, prc, pblk, cpart, crecv, codes,
                 w_s, a_s, a_r, l_s, l_r, ch_s, ch_r, la_s, la_r, p_s, p_r, st_s, st_r, iv_s, iv_r, tq_s, tq_r, tc_s, tc_r, h_s, h_r,
                 lr_s, lr_r, g_s, g_r, t_s, t_r, pp_s, pp_r, pb_s, pb_r, c_s, c_r, o_s, o_r):
    nq, nc, r, nreal, tq, tb, nch, cw, d_all = dims
    q = lax.axis_index("query")
    c = lax.axis_index("corpus")
    g = c // r
    j = lax.rem(c, r)
    slots, w = hid.shape[0], hid.shape[1]
    total = nq * slots
    nqueries = total // SEQ
    bw = code.shape[1] // nq

    loads = []
    for i, (s, d) in enumerate(((gate_h, gate), (up_h, up), (down_h, down), (code_h, code), (corp_h, corp))):
        cp = pltpu.make_async_copy(s, d, w_s.at[i])
        cp.start()
        loads.append(cp)

    def rq(k):
        return lax.rem(q + k, nq)

    def rc(k):
        return lax.rem(c + k, nc)

    def lane(k):
        return lax.rem(j + k, r)

    barrier = pltpu.get_barrier_semaphore()
    for k in range(1, nq):
        pl.semaphore_signal(barrier, inc=1, device_id=(rq(k), c), device_id_type=pl.DeviceIdType.MESH)
    for k in range(1, nc):
        pl.semaphore_signal(barrier, inc=1, device_id=(q, rc(k)), device_id_type=pl.DeviceIdType.MESH)
    pl.semaphore_wait(barrier, nq - 1 + nc - 1)

    for k in range(1, nq):
        rcopy(lens, lens_all.at[q], l_s.at[k], l_r.at[q], (rq(k), c)).start()

    @pl.when(q != g)
    def _():
        rcopy(hid, colbuf.at[q], a_s, a_r.at[q], (g, c)).start()

    squares = jnp.square(hid[...].astype(F32))
    st_send[...] = lax.dot_general(jnp.ones((8, w), F32), squares, (((1,), (1,)), ((), ())),
                                   precision=lax.Precision.HIGHEST, preferred_element_type=F32)
    for k in range(1, nc):
        rcopy(st_send, st_recv.at[c], st_s.at[k], st_r.at[c], (q, rc(k))).start()
    st_recv[c] = st_send[...]
    lens_all[q] = lens[...]
    for k in range(1, nq):
        s = rq(k)
        rcopy(lens, lens_all.at[s], l_s.at[k], l_r.at[s], (s, c)).wait_recv()
    lens_row = jnp.concatenate([lens_all[i] for i in range(nq)], axis=1)
    slot = lax.broadcasted_iota(jnp.int32, (8, total), 1)
    valid = lax.rem(slot, SEQ) < lens_row
    before = lax.broadcasted_iota(jnp.int32, (total, total), 0) < lax.broadcasted_iota(jnp.int32, (total, total), 1)
    pos = mm(valid.astype(F32).astype(BF16), before.astype(F32).astype(BF16)).astype(jnp.int32)
    pos = jnp.where(valid, pos, -1)[:1]

    for k in range(1, nc):
        s = rc(k)
        rcopy(st_send, st_recv.at[s], st_s.at[k], st_r.at[s], (q, s)).wait_recv()
    stat = st_recv[0]
    for i in range(1, nc):
        stat = stat + st_recv[i]
    inv_all[q] = lax.rsqrt(stat / d_all + epsilon)
    for k in range(1, nq):
        rcopy(inv_all.at[q], inv_all.at[q], iv_s.at[k], iv_r.at[q], (rq(k), c)).start()

    nb = ch_r.shape[0]
    ct = nreal // nb

    def chunk(i, slot_j):
        return xall.at[slot_j, pl.ds(i * ct, ct)]

    def down_chain(i):
        return rcopy(chunk(i, j), chunk(i, j), ch_s.at[0, i], ch_r.at[i], (q, jnp.maximum(c - r, 0)))

    def up_chain(i):
        return rcopy(chunk(i, j), chunk(i, j), ch_s.at[1, i], ch_r.at[i], (q, jnp.minimum(c + r, nc - 1)))

    sends_up = jnp.logical_and(g >= q, g < nc // r - 1)
    sends_down = jnp.logical_and(g <= q, g > 0)

    @pl.when(q == g)
    def _():
        colbuf[q] = hid[...]
        for k in range(1, nq):
            s = rq(k)
            rcopy(hid, colbuf.at[s], a_s, a_r.at[s], (s, c)).wait_recv()
        stacked = colbuf[...].reshape(total, w)
        for i in range(nq):
            row = lax.broadcasted_iota(jnp.int32, (tq, total), 0) + i * tq
            pick = (pos == row).astype(F32).astype(BF16)
            xall[j, i * tq:(i + 1) * tq, :] = mm(pick, stacked).astype(BF16)

    for i in range(nb):
        @pl.when(q != g)
        def _(i=i):
            up_chain(i).wait_recv()

        @pl.when(sends_up)
        def _(i=i):
            up_chain(i).start()

        @pl.when(sends_down)
        def _(i=i):
            down_chain(i).start()

        for k in range(1, r):
            rcopy(chunk(i, j), chunk(i, j), la_s.at[k, i], la_r.at[j, i], (q, g * r + lane(k))).start()
    for k in range(1, nq):
        s = rq(k)
        rcopy(inv_all.at[s], inv_all.at[s], iv_s.at[k], iv_r.at[s], (s, c)).wait_recv()
    inv_row = jnp.concatenate([inv_all[i] for i in range(nq)], axis=1)[:1]
    inv_cols = []
    for i in range(nq):
        row = lax.broadcasted_iota(jnp.int32, (tq, total), 0) + i * tq
        inv_cols.append(jnp.sum(jnp.where(pos == row, inv_row, 0.0), axis=1, keepdims=True))
    inv = jnp.concatenate(inv_cols, axis=0)
    for i in range(nb):
        for k in range(1, r):
            s = lane(k)
            rcopy(chunk(i, s), chunk(i, s), la_s.at[k, i], la_r.at[s, i], (q, g * r + s)).wait_recv()

    loads[0].wait()
    loads[1].wait()

    for i in range(r):
        xn[i] = (xall[i].astype(F32) * inv).astype(BF16)

    side_a = q + 1 - 2 * lax.rem(q, 2)
    side_b = q + 2 - 4 * (q // 2)
    far = nq - 1 - q

    def sides(n):
        odd = lax.rem(n, 2)
        return side_a + (side_b - side_a) * odd, side_b + (side_a - side_b) * odd

    def near_part(n):
        one, _ = sides(n)
        return rcopy(psend.at[n, one], precv.at[n, 0], p_s.at[n, 0], p_r.at[n, 0], (one, c))

    def far_part(n):
        one, _ = sides(n)
        return rcopy(psend.at[n, far], precv.at[n, 1], p_s.at[n, 1], p_r.at[n, 1], (one, c))

    def passed_part(n):
        _, two = sides(n)
        return rcopy(precv.at[n, 3], precv.at[n, 2], p_s.at[n, 2], p_r.at[n, 2], (two, c))

    def h_near(n, k):
        to = sides(n)[k]
        return rcopy(hall.at[n, q], hall.at[n, q], h_s.at[n, k], h_r.at[n, k], (to, c))

    def h_near_in(n, k):
        to = sides(n)[k]
        return rcopy(hall.at[n, to], hall.at[n, to], h_s.at[n, k], h_r.at[n, k], (to, c))

    def h_pass(n):
        one, two = sides(n)
        return rcopy(hall.at[n, one], hall.at[n, one], h_s.at[n, 2], h_r.at[n, 2], (two, c))

    def h_pass_in(n):
        _, two = sides(n)
        return rcopy(hall.at[n, far], hall.at[n, far], h_s.at[n, 2], h_r.at[n, 2], (two, c))

    def matmuls(n, carry):
        cols = pl.ds(pl.multiple_of(n * cw, cw), cw)
        for e, wref in enumerate((gate, up)):
            full = sum(mm(xn[i], wref[i * w:(i + 1) * w, cols]) for i in range(r))
            for i in range(nq):
                psend[n, i, e] = full[i * tq:(i + 1) * tq].astype(BF16)

                @pl.when(q == i)
                def _(i=i, e=e, full=full):
                    pown[n, e] = full[i * tq:(i + 1) * tq]
        far_part(n).start()
        near_part(n).start()
        return carry

    lax.fori_loop(0, nch, matmuls, 0)

    loads[2].wait()
    acc[...] = jnp.zeros_like(acc)

    def pass_chunk(n):
        _, two = sides(n)
        far_part(n).wait_recv()
        precv[n, 3] = (psend[n, two].astype(F32) + precv[n, 1].astype(F32)).astype(BF16)
        passed_part(n).start()

    def reduce_chunk(n):
        near_part(n).wait_recv()
        passed_part(n).wait_recv()
        gsum = pown[n, 0] + precv[n, 0, 0].astype(F32) + precv[n, 2, 0].astype(F32)
        usum = pown[n, 1] + precv[n, 0, 1].astype(F32) + precv[n, 2, 1].astype(F32)
        hall[n, q] = (gsum / (1.0 + jnp.exp(-gsum)) * usum).astype(BF16)
        h_near(n, 0).start()
        h_near(n, 1).start()

    def relay_chunk(n):
        h_near_in(n, 0).wait_recv()
        h_pass(n).start()

    def down_chunk(n):
        h_near_in(n, 1).wait_recv()
        h_pass_in(n).wait_recv()
        acc[...] += mm(hall[n].reshape(nreal, cw), down[pl.ds(pl.multiple_of(n * cw, cw), cw), :])

    def passes(n, carry):
        pass_chunk(n)
        return carry

    lax.fori_loop(0, nch, passes, 0)
    reduce_chunk(0)

    def reduces(n, carry):
        reduce_chunk(n)
        relay_chunk(n - 1)
        return carry

    lax.fori_loop(1, nch, reduces, 0)
    relay_chunk(nch - 1)

    def downs(n, carry):
        down_chunk(n)
        return carry

    lax.fori_loop(0, nch, downs, 0)

    ng = nc // r
    for gg in range(ng):
        for jj in range(r):
            b = gg * r + jj
            lsend[jj, gg] = acc[b * tb:(b + 1) * tb].astype(BF16)
    for k in range(1, r):
        t = lane(k)
        rcopy(lsend.at[t], lrecv.at[j], lr_s.at[k], lr_r.at[j], (q, g * r + t)).start()
    mine = lsend[j].astype(F32)
    for k in range(1, r):
        s = lane(k)
        rcopy(lsend.at[s], lrecv.at[s], lr_s.at[k], lr_r.at[s], (q, g * r + s)).wait_recv()
        mine = mine + lrecv[s].astype(F32)
    gsend[...] = mine.astype(BF16)
    for k in range(1, ng):
        t = lax.rem(g + k, ng)
        rcopy(gsend.at[t], grecv.at[g], g_s.at[k], g_r.at[g], (q, t * r + j)).start()
    row = lax.broadcasted_iota(jnp.int32, (tb, nreal), 0) + c * tb
    own_rows = (lax.broadcasted_iota(jnp.int32, (tb, nreal), 1) == row).astype(F32).astype(BF16)
    residual = jnp.concatenate([mm(own_rows, xall[i]) for i in range(r)], axis=1)
    residual = residual + gsend[g].astype(F32)
    for k in range(1, ng):
        s = lax.rem(g + k, ng)
        rcopy(gsend.at[s], grecv.at[s], g_s.at[k], g_r.at[s], (q, s * r + j)).wait_recv()
        residual = residual + grecv[s].astype(F32)

    t_send[...] = jnp.broadcast_to(jnp.sum(residual * residual, axis=1, keepdims=True), (tb, 128))
    for k in range(1, nq):
        rcopy(t_send, t_recv.at[q], t_s.at[k], t_r.at[q], (rq(k), c)).start()
    qrow = lax.broadcasted_iota(jnp.int32, (nqueries, total), 0)
    qslot = lax.broadcasted_iota(jnp.int32, (nqueries, total), 1)
    lens_b = jnp.broadcast_to(lens_row[:1], (nqueries, total)).astype(F32)
    vals_b = jnp.broadcast_to(valid.astype(F32)[:1], (nqueries, total))
    len_col = jnp.sum(jnp.where(qslot == qrow * SEQ, lens_b, 0.0), axis=1, keepdims=True)
    off_col = jnp.sum(jnp.where(qslot < qrow * SEQ, vals_b, 0.0), axis=1, keepdims=True)
    prow = (lax.broadcasted_iota(jnp.int32, (nqueries, tb), 1) + c * tb).astype(F32)
    member = jnp.where(jnp.logical_and(prow >= off_col, prow < off_col + len_col), 1.0, 0.0)
    tsum = t_send[...]
    for k in range(1, nq):
        s = rq(k)
        rcopy(t_send, t_recv.at[s], t_s.at[k], t_r.at[s], (s, c)).wait_recv()
        tsum = tsum + t_recv[s]
    final = residual * lax.rsqrt(tsum[:, :1] / d_all + epsilon)
    pooled_part = mm(member, final, lax.Precision.HIGHEST)
    for i in range(r):
        pp[i] = pooled_part[:, i * w:(i + 1) * w]
    for i in range(r):
        @pl.when(c != q * r + i)
        def _(i=i):
            rcopy(pp.at[i], prc.at[c], pp_s.at[i], pp_r.at[c], (q, q * r + i)).start()

    @pl.when(g == q)
    def _():
        pooled = pp[j]
        for k in range(1, nc):
            s = rc(k)
            rcopy(pp.at[j], prc.at[s], pp_s.at[0], pp_r.at[s], (q, s)).wait_recv()
            pooled = pooled + prc[s]
        pblk[...] = (pooled / len_col).astype(BF16)
        for k in range(1, nq):
            rcopy(pblk, pblk, pb_s.at[k], pb_r, (rq(k), c)).start()

    loads[3].wait()
    loads[4].wait()

    @pl.when(g != q)
    def _():
        rcopy(pblk, pblk, pb_s.at[0], pb_r, (g, c)).wait_recv()

    cpart[...] = mm(pblk[...], code[:, pl.ds(pl.multiple_of(q * bw, bw), bw)])
    for k in range(1, nc):
        rcopy(cpart, crecv.at[c], c_s.at[k], c_r.at[c], (q, rc(k))).start()
    crecv[c] = cpart[...]
    for k in range(1, nc):
        s = rc(k)
        rcopy(cpart, crecv.at[s], c_s.at[k], c_r.at[s], (q, s)).wait_recv()
    csum = crecv[0]
    for i in range(1, nc):
        csum = csum + crecv[i]
    codes[q] = csum.astype(BF16)
    for k in range(1, nq):
        rcopy(codes.at[q], codes.at[q], o_s.at[k], o_r.at[q], (rq(k), c)).start()
    for k in range(1, nq):
        s = rq(k)
        rcopy(codes.at[s], codes.at[s], o_s.at[k], o_r.at[s], (s, c)).wait_recv()
    qcodes = jnp.concatenate([codes[i] for i in range(nq)], axis=1)
    scale = 1.0 / math.sqrt(corp.shape[1])
    scores = lax.dot_general(qcodes, corp[...], (((1,), (1,)), ((), ())), preferred_element_type=F32) * scale

    blocks = corp.shape[0] // LANES
    lists = jnp.concatenate([scores[:, i * LANES:(i + 1) * LANES] for i in range(blocks)], axis=0)
    best = merge_all(sort_lanes(lists), nqueries, q >= nq // 2)
    top_q[q] = best
    for k in range(1, nq):
        rcopy(top_q.at[q], top_q.at[q], tq_s.at[k], tq_r.at[q], (rq(k), c)).start()
    for k in range(1, nq):
        s = rq(k)
        rcopy(top_q.at[s], top_q.at[s], tq_s.at[k], tq_r.at[s], (s, c)).wait_recv()
    best = merge_all(top_q[...].reshape(nq * nqueries, LANES), nqueries, c >= nc // 2)
    top_c[c] = best
    for k in range(1, nc):
        rcopy(top_c.at[c], top_c.at[c], tc_s.at[k], tc_r.at[c], (q, rc(k))).start()
    for k in range(1, nc):
        s = rc(k)
        rcopy(top_c.at[s], top_c.at[s], tc_s.at[k], tc_r.at[s], (q, s)).wait_recv()
    best = merge_all(top_c[...].reshape(nc * nqueries, LANES), nqueries, False)
    out[...] = best[:, :TOPK]

    for k in range(1, nq):
        rcopy(lens, lens_all.at[q], l_s.at[k], l_r.at[q], (rq(k), c)).wait_send()
        rcopy(inv_all.at[q], inv_all.at[q], iv_s.at[k], iv_r.at[q], (rq(k), c)).wait_send()
        rcopy(top_q.at[q], top_q.at[q], tq_s.at[k], tq_r.at[q], (rq(k), c)).wait_send()
        rcopy(t_send, t_recv.at[q], t_s.at[k], t_r.at[q], (rq(k), c)).wait_send()
        rcopy(codes.at[q], codes.at[q], o_s.at[k], o_r.at[q], (rq(k), c)).wait_send()

    @pl.when(q != g)
    def _():
        rcopy(hid, colbuf.at[q], a_s, a_r.at[q], (g, c)).wait_send()

    for i in range(nb):
        @pl.when(sends_up)
        def _(i=i):
            up_chain(i).wait_send()

        @pl.when(sends_down)
        def _(i=i):
            down_chain(i).wait_send()

        for k in range(1, r):
            rcopy(chunk(i, j), chunk(i, j), la_s.at[k, i], la_r.at[j, i], (q, g * r + lane(k))).wait_send()

    def drain(n, carry):
        far_part(n).wait_send()
        near_part(n).wait_send()
        passed_part(n).wait_send()
        h_near(n, 0).wait_send()
        h_near(n, 1).wait_send()
        h_pass(n).wait_send()
        return carry

    lax.fori_loop(0, nch, drain, 0)
    for k in range(1, r):
        rcopy(lsend.at[lane(k)], lrecv.at[j], lr_s.at[k], lr_r.at[j], (q, g * r + lane(k))).wait_send()
    for k in range(1, ng):
        t = lax.rem(g + k, ng)
        rcopy(gsend.at[t], grecv.at[g], g_s.at[k], g_r.at[g], (q, t * r + j)).wait_send()
    for i in range(r):
        @pl.when(c != q * r + i)
        def _(i=i):
            rcopy(pp.at[i], prc.at[c], pp_s.at[i], pp_r.at[c], (q, q * r + i)).wait_send()

    @pl.when(g == q)
    def _():
        for k in range(1, nq):
            rcopy(pblk, pblk, pb_s.at[k], pb_r, (rq(k), c)).wait_send()
    for k in range(1, nc):
        rcopy(cpart, crecv.at[c], c_s.at[k], c_r.at[c], (q, rc(k))).wait_send()
        rcopy(st_send, st_recv.at[c], st_s.at[k], st_r.at[c], (q, rc(k))).wait_send()
        rcopy(top_c.at[c], top_c.at[c], tc_s.at[k], tc_r.at[c], (q, rc(k))).wait_send()


def per_device(nq, nc, hidden_in, lengths, gate_weight, up_weight, down_weight, code_weight, corpus_codes):
    slots, w = hidden_in.shape
    r = nc // nq
    nreal = nq * slots * REAL_NUM // REAL_DEN
    tq, tb = nreal // nq, nreal // nc
    dq, ffc = gate_weight.shape
    cw = CHUNK if ffc % CHUNK == 0 else ffc
    nch = ffc // cw
    nb = nreal // PIECE if nreal % PIECE == 0 else nq
    nqueries = nq * lengths.shape[0]
    bits = code_weight.shape[1]
    bw = bits // nq
    ng = nc // r
    lens = jnp.broadcast_to(jnp.repeat(lengths, SEQ)[None, :], (8, slots))
    vm, dma = pltpu.VMEM, pltpu.SemaphoreType.DMA
    scratch = [
        vm(gate_weight.shape, BF16), vm(up_weight.shape, BF16), vm(down_weight.shape, BF16),
        vm(code_weight.shape, BF16), vm(corpus_codes.shape, BF16),
        vm((nq, slots, w), BF16), vm((nq, 8, slots), jnp.int32), vm((r, nreal, w), BF16),
        vm((nch, nq, 2, tq, cw), BF16), vm((nch, nq, 2, tq, cw), BF16),
        vm((8, slots), F32), vm((nc, 8, slots), F32), vm((nq, 8, slots), F32), vm((r, nreal, w), BF16),
        vm((nch, 2, tq, cw), F32), vm((nq, nqueries, LANES), F32), vm((nc, nqueries, LANES), F32),
        vm((nch, nq, tq, cw), BF16), vm((nreal, dq), F32),
        vm((r, ng, tb, dq), BF16), vm((r, ng, tb, dq), BF16), vm((ng, tb, dq), BF16), vm((ng, tb, dq), BF16),
        vm((tb, 128), F32), vm((nq, tb, 128), F32),
        vm((r, nqueries, w), F32), vm((nc, nqueries, w), F32), vm((nqueries, w), BF16),
        vm((nqueries, bw), F32), vm((nc, nqueries, bw), F32), vm((nq, nqueries, bw), BF16),
        dma((5,)), dma, dma((nq,)), dma((nq,)), dma((nq,)), dma((2, nb)), dma((nb,)), dma((r, nb)), dma((r, nb)),
        dma((nch, nq)), dma((nch, nq)), dma((nc,)), dma((nc,)), dma((nq,)), dma((nq,)),
        dma((nq,)), dma((nq,)), dma((nc,)), dma((nc,)), dma((nch, nq)), dma((nch, nq)),
        dma((r,)), dma((r,)), dma((ng,)), dma((ng,)), dma((nq,)), dma((nq,)),
        dma((r,)), dma((nc,)), dma((nq,)), dma, dma((nc,)), dma((nc,)), dma((nq,)), dma((nq,)),
    ]
    dims = (nq, nc, r, nreal, tq, tb, nch, cw, w * nc)
    vspec, aspec = pl.BlockSpec(memory_space=pltpu.VMEM), pl.BlockSpec(memory_space=pl.ANY)
    return pl.pallas_call(
        functools.partial(block_kernel, dims),
        out_shape=jax.ShapeDtypeStruct((nqueries, TOPK), F32),
        in_specs=[vspec, vspec] + [aspec] * 5,
        out_specs=vspec,
        scratch_shapes=scratch,
        compiler_params=pltpu.CompilerParams(
            collective_id=0, has_side_effects=True, vmem_limit_bytes=60 * 1024 * 1024),
    )(hidden_in, lens, gate_weight, up_weight, down_weight, code_weight, corpus_codes)


def solution(mesh):
    in_specs = (
        P("query", "corpus"),
        P("query"),
        P("query", "corpus"),
        P("query", "corpus"),
        P("corpus", "query"),
        P("corpus", None),
        P(("query", "corpus"), None),
    )
    body = functools.partial(per_device, mesh.shape["query"], mesh.shape["corpus"])
    return jax.shard_map(body, mesh=mesh, in_specs=in_specs, out_specs=P(), check_vma=False)
```
